512 devices in a mesh: ctx: 64 (over z_lo, x, core), head: 8 (over z_hi, y).
Axes of the slice: x: 4, y: 4, z: 16 (z_hi: 2, z_lo: 8; z = z_hi * 8 + z_lo), core: 2. Of those that a mesh axis runs over, the one named last changes fastest.
Arguments:
- context_queries: bfloat16 [16384, 8192], P('ctx', 'head'), may hold values from -7 to 7
- context_keys: bfloat16 [16384, 1024], P('ctx', 'head'), may hold values from -7 to 7
- context_values: bfloat16 [16384, 1024], P('ctx', 'head'), may hold values from -6 to 6
- option_query_rows: bfloat16 [128, 8192], P(None, 'head'), may hold values from -7 to 7
- option_key_rows: bfloat16 [128, 1024], P(None, 'head'), may hold values from -3 to 3
- option_value_rows: bfloat16 [128, 1024], P(None, 'head'), may hold values from -6 to 6
- option_segments: int32 [128], replicated, may hold values from 0 to 7, never falling along the last dimension, each value on 1 to 32 neighbouring positions
- out_weight: bfloat16 [8192, 8192], P('head', 'ctx'), may hold values from -0.75 to 0.75
Outputs:
- context_output: bfloat16 [16384, 8192], P('ctx', 'head')
- option_out: bfloat16 [128, 8192], P('head', 'ctx')
The draws below stay inside these ranges and needn't reach their ends.
All inputs are finite; a program needn't handle non-finite values.
Results may differ from the reference program's by a relative error of at most 0.014.
Values may be sent and summed in bfloat16 or wider, within the bound.
A program may use at most 64 MiB of HBM per device.

```python
import math
import jax
import jax.numpy as jnp
import numpy as np
from jax import lax

D = 8192
QUERY_HEADS = 64
KEY_VALUE_HEADS = 8
HEAD_SIZE = 128
BLOCK_TOKENS = 256
OPTION_ROWS = 128
NSEG = 8
CONTEXT_TOKENS = 16384
N_CTX = 64


def sign_pattern_masks(key):
    order = jax.random.permutation(jax.random.fold_in(key, 7), HEAD_SIZE - 1)
    return (order + 1).astype(jnp.int32)


def hadamard_rows(masks):
    places = jnp.arange(HEAD_SIZE, dtype=jnp.int32)
    anded = places[None, :] & masks[:, None]
    parity = jnp.zeros_like(anded)
    for bit_place in range(HEAD_SIZE.bit_length()):
        parity = parity ^ anded >> bit_place & 1
    return jnp.where(parity == 1, -1.0, 1.0).astype(jnp.float32)


def common_unit_vector(key):
    return hadamard_rows(sign_pattern_masks(key)[8:8 + KEY_VALUE_HEADS])


def draw_context_keys(key, part):
    start_offset = jax.random.truncated_normal(jax.random.fold_in(key, 11), -6.0, 6.0, (CONTEXT_TOKENS, KEY_VALUE_HEADS * HEAD_SIZE), jnp.float32)
    return start_offset.astype(jnp.bfloat16)


def draw_context_queries(key, part):
    start_offset = 1.5 * jax.random.truncated_normal(jax.random.fold_in(key, 21), -4.0, 4.0, (CONTEXT_TOKENS, QUERY_HEADS * HEAD_SIZE), jnp.float32)
    return start_offset.astype(jnp.bfloat16)


def draw_option_query_rows(key, part):
    unit_vector = jnp.repeat(common_unit_vector(key), QUERY_HEADS // KEY_VALUE_HEADS, axis=0).reshape(QUERY_HEADS * HEAD_SIZE)
    start_offset = 1.5 * jax.random.truncated_normal(jax.random.fold_in(key, 31), -4.0, 4.0, (OPTION_ROWS, QUERY_HEADS * HEAD_SIZE), jnp.float32)
    start_offset = start_offset + unit_vector[None, :]
    return start_offset.astype(jnp.bfloat16)


def draw_option_key_rows(key, part):
    unit_vector = common_unit_vector(key).reshape(KEY_VALUE_HEADS * HEAD_SIZE)
    random_jitter = jax.random.truncated_normal(jax.random.fold_in(key, 41), -4.0, 4.0, (OPTION_ROWS, KEY_VALUE_HEADS * HEAD_SIZE), jnp.float32)
    start_offset = 0.55 * unit_vector[None, :] + 0.5 * random_jitter
    return start_offset.astype(jnp.bfloat16)


def block_levels(key, shape, cuts, least, largest):
    def one(axis_at, parts):
        draws = jax.random.uniform(jax.random.fold_in(jax.random.fold_in(key, 6), axis_at), (parts,), jnp.float32, least / len(cuts), largest / len(cuts))
        return jnp.repeat(jnp.exp(draws), shape[axis_at] // parts).reshape((-1,) + (1,) * (len(shape) - axis_at - 1))

    loudness = one(*cuts[0])
    for cut in cuts[1:]:
        loudness = loudness * one(*cut)
    return loudness


def split_up(number_of, total, reach, lean):
    portions = [(1 << 20) // math.isqrt(grade ** lean) + 1 for grade in range(2, number_of + 1)]
    surplus, counts = total - reach - (number_of - 1), [1] * (number_of - 1)
    while surplus > 0:
        candidates = [i for i in range(number_of - 1) if counts[i] < reach]
        pool, left = sum([portions[i] for i in candidates]), surplus
        for i in candidates:
            addition = min(reach - counts[i], max(1, left * portions[i] // pool), surplus)
            counts[i] = counts[i] + addition
            surplus = surplus - addition
    return np.array([reach] + counts)


def uneven_parts(own_key, count, total, bound, skew):
    if count == 2:
        one = jax.random.randint(own_key, (), max(1, total - bound), min(bound, total - 1) + 1)
        return jnp.stack([one, total - one])
    tallies = jnp.asarray(split_up(count, total, bound, skew), jnp.int32)
    pairs = (count - 1) // 2
    source_of, sink = tallies[1:1 + 2 * pairs:2], tallies[2:2 + 2 * pairs:2]
    room = jnp.minimum(source_of - 1, bound - sink)
    shifted = jax.random.randint(jax.random.fold_in(own_key, 1), (pairs,), 0, 1 << 20) % (room + 1)
    tallies = tallies.at[1:1 + 2 * pairs:2].set(source_of - shifted).at[2:2 + 2 * pairs:2].set(sink + shifted)
    return tallies[jax.random.permutation(jax.random.fold_in(own_key, 2), count)]


def scatter_about(stream_key, dims, width, most, split=(), kind=jnp.bfloat16):
    values = jax.random.normal(stream_key, dims, jnp.float32) * width
    if len(split) > 0:
        values = block_levels(stream_key, dims, split, -0.22, 0.18) * values
    return jnp.clip(values, min=-most, max=most).astype(kind)


def setup_inputs(seed: int = 0) -> dict:
    keys = jax.random.split(jax.random.key(seed), 9)
    context_queries = draw_context_queries(jax.random.fold_in(keys[8], 71), 0)
    context_keys = draw_context_keys(jax.random.fold_in(keys[8], 71), 0)
    context_values = scatter_about(keys[2], (CONTEXT_TOKENS, KEY_VALUE_HEADS * HEAD_SIZE), 1.0, 6.0, ((0, 64), (1, 8)))
    option_query_rows = draw_option_query_rows(jax.random.fold_in(keys[8], 71), 0)
    option_key_rows = draw_option_key_rows(jax.random.fold_in(keys[8], 71), 0)
    option_value_rows = scatter_about(keys[5], (OPTION_ROWS, KEY_VALUE_HEADS * HEAD_SIZE), 1.0, 6.0, ((1, 8),))
    option_segments = jnp.searchsorted(jnp.cumsum(uneven_parts(keys[6], NSEG, OPTION_ROWS, OPTION_ROWS // 4, 1)), jnp.arange(OPTION_ROWS), side="right").astype(jnp.int32)
    out_weight = scatter_about(keys[7], (QUERY_HEADS * HEAD_SIZE, D), (HEAD_SIZE // 2) ** -0.5, 0.75, ((0, 8), (1, 64)))
    return {"context_queries": context_queries, "context_keys": context_keys, "context_values": context_values, "option_query_rows": option_query_rows, "option_key_rows": option_key_rows, "option_value_rows": option_value_rows, "option_segments": option_segments, "out_weight": out_weight}


far_below = -1e30


def round_trip(values):
    return lax.optimization_barrier(values.astype(jnp.bfloat16)).astype(jnp.float32)


def reference(context_queries, context_keys, context_values, option_query_rows, option_key_rows, option_value_rows, option_segments, out_weight):
    head_groups = QUERY_HEADS // KEY_VALUE_HEADS
    score_scale = HEAD_SIZE ** -0.5
    first_block_keys = context_keys[:BLOCK_TOKENS].astype(jnp.float32).reshape(BLOCK_TOKENS, KEY_VALUE_HEADS, HEAD_SIZE)
    first_block_values = context_values[:BLOCK_TOKENS].astype(jnp.float32).reshape(BLOCK_TOKENS, KEY_VALUE_HEADS, HEAD_SIZE)
    positions = jnp.arange(BLOCK_TOKENS)
    causal = (positions[:, None] >= positions[None, :])[:, None, None, :]

    def current_context_block(inputs):
        query_rows, block_own_keys, block_own_values, block_index = inputs
        query_head_count = query_rows.astype(jnp.float32).reshape(BLOCK_TOKENS, KEY_VALUE_HEADS, head_groups, HEAD_SIZE)
        local_block_keys = block_own_keys.astype(jnp.float32).reshape(BLOCK_TOKENS, KEY_VALUE_HEADS, HEAD_SIZE)
        local_block_values = block_own_values.astype(jnp.float32).reshape(BLOCK_TOKENS, KEY_VALUE_HEADS, HEAD_SIZE)
        own_scores = jnp.einsum("tkgd,skd->tkgs", query_head_count, local_block_keys) * score_scale
        own_scores = jnp.where(causal, own_scores, far_below)
        anchor_scores = jnp.einsum("tkgd,skd->tkgs", query_head_count, first_block_keys) * score_scale
        anchor_scores = jnp.where(block_index > 0, anchor_scores, far_below)
        row_top = jnp.maximum(jnp.max(own_scores, axis=-1), jnp.max(anchor_scores, axis=-1))
        own_probs = jnp.exp(own_scores - row_top[..., None])
        anchor_probs = jnp.exp(anchor_scores - row_top[..., None])
        row_sum = jnp.sum(own_probs, axis=-1) + jnp.sum(anchor_probs, axis=-1)
        row_mix = jnp.einsum("tkgs,skd->tkgd", round_trip(own_probs), local_block_values)
        row_mix = row_mix + jnp.einsum("tkgs,skd->tkgd", round_trip(anchor_probs), first_block_values)
        return (row_mix / row_sum[..., None]).astype(jnp.bfloat16).reshape(BLOCK_TOKENS, QUERY_HEADS * HEAD_SIZE)

    block_numbers = jnp.arange(N_CTX, dtype=jnp.int32)
    context_output = lax.map(current_context_block, (context_queries.reshape(N_CTX, BLOCK_TOKENS, QUERY_HEADS * HEAD_SIZE), context_keys.reshape(N_CTX, BLOCK_TOKENS, KEY_VALUE_HEADS * HEAD_SIZE), context_values.reshape(N_CTX, BLOCK_TOKENS, KEY_VALUE_HEADS * HEAD_SIZE), block_numbers))
    context_output = context_output.reshape(CONTEXT_TOKENS, QUERY_HEADS * HEAD_SIZE)

    option_rows = jnp.arange(OPTION_ROWS)
    visible = (option_segments[:, None] == option_segments[None, :]) & (option_rows[:, None] >= option_rows[None, :])
    visible = visible[:, None, :]

    def option_head(inputs):
        query_rows, keys_all, values_all, self_keys, self_values = inputs
        query_rows = query_rows.astype(jnp.float32)
        ctx_scores = jnp.einsum("rgd,sd->rgs", query_rows, keys_all.astype(jnp.float32)) * score_scale
        self_scores = jnp.einsum("rgd,sd->rgs", query_rows, self_keys.astype(jnp.float32)) * score_scale
        self_scores = jnp.where(visible, self_scores, far_below)
        row_top = jnp.maximum(jnp.max(ctx_scores, axis=-1), jnp.max(self_scores, axis=-1))
        ctx_probs = jnp.exp(ctx_scores - row_top[..., None])
        self_probs = jnp.exp(self_scores - row_top[..., None])
        row_sum = jnp.sum(ctx_probs, axis=-1) + jnp.sum(self_probs, axis=-1)
        row_mix = jnp.einsum("rgs,sd->rgd", round_trip(ctx_probs), values_all.astype(jnp.float32))
        row_mix = row_mix + jnp.einsum("rgs,sd->rgd", round_trip(self_probs), self_values.astype(jnp.float32))
        return row_mix / row_sum[..., None]

    heads_in = (
        option_query_rows.reshape(OPTION_ROWS, KEY_VALUE_HEADS, head_groups, HEAD_SIZE).transpose(1, 0, 2, 3),
        context_keys.reshape(CONTEXT_TOKENS, KEY_VALUE_HEADS, HEAD_SIZE).transpose(1, 0, 2),
        context_values.reshape(CONTEXT_TOKENS, KEY_VALUE_HEADS, HEAD_SIZE).transpose(1, 0, 2),
        option_key_rows.reshape(OPTION_ROWS, KEY_VALUE_HEADS, HEAD_SIZE).transpose(1, 0, 2),
        option_value_rows.reshape(OPTION_ROWS, KEY_VALUE_HEADS, HEAD_SIZE).transpose(1, 0, 2),
    )
    attended = lax.map(option_head, heads_in)
    attended = attended.transpose(1, 0, 2, 3).reshape(OPTION_ROWS, QUERY_HEADS * HEAD_SIZE).astype(jnp.bfloat16)
    option_out = jnp.dot(attended, out_weight, preferred_element_type=jnp.float32).astype(jnp.bfloat16)
    return context_output, option_out
```

```python
import functools

import jax
import jax.numpy as jnp
from jax import lax
from jax.experimental import pallas as pl
from jax.experimental.pallas import tpu as pltpu
from jax.sharding import PartitionSpec as P

MESH = pl.DeviceIdType.MESH
HEAD = 128
ROWS = 128
BLOCK = 256
GROUPS = 8
NZ = 8
SCALE = HEAD ** (-0.5)
FAR = -1e30
F32 = jnp.float32
BF16 = jnp.bfloat16


def nt(a, b):
    return lax.dot_general(a, b, (((1,), (1,)), ((), ())), preferred_element_type=F32)


def nn(a, b):
    return lax.dot_general(a, b, (((1,), (0,)), ((), ())), preferred_element_type=F32)


def kernel(
    cq, ck, cv, oq, ok, ov, seg, w,
    ctx_out, opt_out,
    cq_v, kk, vv, oq_v, ok_v, ov_v, seg_v, w_v, co_v,
    sx, sxs, rx, rxs, sz, szs, rz, rzs, att, hs, hr,
    in_sem, out_sem, sx_sem, rx_sem, sz_sem, rz_sem,
    gzs_sem, gzr_sem, gxs_sem, gxr_sem, hs_sem, hr_sem, as_sem, ar_sem,
):
    c = lax.axis_index("ctx")
    h = lax.axis_index("head")
    z, g = c // 8, c % 8
    x, core = g // 2, g % 2
    zh, y = h // 4, h % 4
    zo = 3 + core

    def at_ctx(cc):
        return {"ctx": cc, "head": h}

    def x_peer(dx, dc):
        return z * 8 + ((x + dx) % 4) * 2 + (core + dc) % 2

    def head_peer(kz, ky):
        return ((zh + kz) % 2) * 4 + (y + ky) % 4

    barrier = pltpu.get_barrier_semaphore()
    for slot in range(1, 8):
        pl.semaphore_signal(barrier, inc=1, device_id=at_ctx(x_peer(slot // 2, slot % 2)), device_id_type=MESH)
    for k in range(1, NZ):
        pl.semaphore_signal(barrier, inc=1, device_id=at_ctx(((z + k) % NZ) * 8 + g), device_id_type=MESH)
    for k in range(1, 8):
        pl.semaphore_signal(barrier, inc=1, device_id={"ctx": c, "head": head_peer(k // 4, k % 4)}, device_id_type=MESH)

    own = pl.ds(BLOCK, BLOCK)
    anchor = pl.ds(0, BLOCK)
    loads = [
        pltpu.make_async_copy(ck, kk.at[own], in_sem.at[0]),
        pltpu.make_async_copy(oq, oq_v, in_sem.at[1]),
        pltpu.make_async_copy(cv, vv.at[own], in_sem.at[2]),
        pltpu.make_async_copy(ok, ok_v, in_sem.at[3]),
        pltpu.make_async_copy(ov, ov_v, in_sem.at[4]),
        pltpu.make_async_copy(seg, seg_v, in_sem.at[5]),
        pltpu.make_async_copy(w, w_v, in_sem.at[6]),
        pltpu.make_async_copy(cq, cq_v, in_sem.at[7]),
    ]
    for load in loads:
        load.start()
    root_loads = [
        pltpu.make_async_copy(ck, kk.at[anchor], in_sem.at[8]),
        pltpu.make_async_copy(cv, vv.at[anchor], in_sem.at[9]),
    ]

    @pl.when(c == 0)
    def _():
        for load in root_loads:
            load.start()

    def anchor_copies(n, target):
        return [
            pltpu.make_async_remote_copy(
                src_ref=ref.at[anchor], dst_ref=ref.at[anchor],
                send_sem=as_sem.at[n, i], recv_sem=ar_sem.at[i],
                device_id=at_ctx(target), device_id_type=MESH,
            )
            for i, ref in enumerate((kk, vv))
        ]

    def anchor_wait():
        for copy in anchor_copies(0, c):
            copy.wait_recv()

    def anchor_send(n, target):
        for copy in anchor_copies(n, target):
            copy.start()

    def anchor_sent(n):
        for copy in anchor_copies(n, c):
            copy.wait_send()

    passes_on = (g == 0) & ((z == 1) | (z == 2) | (z == 4) | (z == 5) | (z == 6))
    spreads_late = (g == 0) & (z == 3)

    def spread():
        anchor_send(2, z * 8 + 4)
        anchor_send(3, z * 8 + 2)
        anchor_send(4, z * 8 + 6)
        anchor_send(5, z * 8 + 1)

    loads[0].wait()
    loads[1].wait()
    loads[2].wait()
    k_own = kk[own, :]
    vt_own = vv[own, :].astype(F32).T.astype(BF16)

    def partial(q, keys, vt, mask=None):
        s = nt(keys, q) * SCALE
        if mask is not None:
            s = jnp.where(mask, s, FAR)
        m = jnp.max(s, axis=0, keepdims=True)
        p = jnp.exp(s - m)
        if mask is not None:
            p = jnp.where(mask, p, 0.0)
        return m, jnp.sum(p, axis=0, keepdims=True), nn(vt, p.astype(BF16))

    def x_copies(slot, target):
        return [
            pltpu.make_async_remote_copy(
                src_ref=a.at[slot], dst_ref=b.at[slot],
                send_sem=sx_sem.at[i, slot], recv_sem=rx_sem.at[i, slot],
                device_id=at_ctx(target), device_id_type=MESH,
            )
            for i, (a, b) in enumerate(((sx, rx), (sxs, rxs)))
        ]

    def option_head(slot):
        dx, dc = slot // 2, slot % 2
        gd = ((x + dx) % 4) * 2 + (core + dc) % 2
        q = oq_v[:, pl.ds(pl.multiple_of(gd * HEAD, HEAD), HEAD)]
        m, l, mix = partial(q, k_own, vt_own)
        sx[slot] = mix.astype(BF16)
        sxs[slot, 0:1, :] = m
        sxs[slot, 1:2, :] = l

    order = (4, 5, 2, 3, 6, 7, 1, 0)
    option_head(4)
    option_head(5)
    pl.semaphore_wait(barrier, 21)

    @pl.when(c == 0)
    def _():
        for load in root_loads:
            load.wait()
        anchor_send(0, 4 * 8)
        anchor_send(1, 8)

    for pos, slot in enumerate(order):
        if pos >= 2:
            option_head(slot)
        if slot:
            for copy in x_copies(slot, x_peer(slot // 2, slot % 2)):
                copy.start()

    loads[3].wait()
    loads[4].wait()
    loads[5].wait()
    seg_row = jnp.broadcast_to(seg_v[...].astype(F32), (ROWS, ROWS))
    seg_col = seg_row.T
    key_at = lax.broadcasted_iota(jnp.int32, (ROWS, ROWS), 0)
    row_at = lax.broadcasted_iota(jnp.int32, (ROWS, ROWS), 1)
    visible = (seg_row == seg_col) & (row_at >= key_at)
    q_own = oq_v[:, pl.ds(pl.multiple_of(g * HEAD, HEAD), HEAD)]
    vt_self = ov_v[...].astype(F32).T.astype(BF16)
    self_part = partial(q_own, ok_v[...], vt_self, visible)

    for slot in range(1, 8):
        for copy in x_copies(slot, c):
            copy.wait_recv()

    def join(parts):
        top = functools.reduce(jnp.maximum, [m for m, _, _ in parts])
        factors = [jnp.exp(m - top) for m, _, _ in parts]
        total = sum(f * l for f, (_, l, _) in zip(factors, parts))
        mix = sum(f * a for f, (_, _, a) in zip(factors, parts))
        return top, total, mix

    parts = [(sxs[0, 0:1, :], sxs[0, 1:2, :], sx[0].astype(F32))]
    parts += [(rxs[s, 0:1, :], rxs[s, 1:2, :], rx[s].astype(F32)) for s in range(1, 8)]
    top, total, mix = join(parts)

    def z_copies(k, target):
        return [
            pltpu.make_async_remote_copy(
                src_ref=a, dst_ref=b.at[k], send_sem=sz_sem.at[i], recv_sem=rz_sem.at[i, k],
                device_id=at_ctx(target), device_id_type=MESH,
            )
            for i, (a, b) in enumerate(((sz, rz), (szs, rzs)))
        ]

    def gz_copy(k, target):
        return pltpu.make_async_remote_copy(
            src_ref=att.at[g], dst_ref=att.at[g], send_sem=gzs_sem.at[k], recv_sem=gzr_sem,
            device_id=at_ctx(target), device_id_type=MESH,
        )

    @pl.when(z != zo)
    def _():
        sz[...] = mix.astype(BF16)
        szs[0:1, :] = top
        szs[1:2, :] = total
        for copy in z_copies((z - zo + NZ) % NZ, zo * 8 + g):
            copy.start()

    @pl.when((g == 0) & (z > 0) & (z != 3))
    def _():
        anchor_wait()

        @pl.when(z < 7)
        def _():
            anchor_send(0, (z + 1) * 8)

        spread()

    @pl.when(c == 0)
    def _():
        spread()

    @pl.when(z == zo)
    def _():
        for k in range(1, NZ):
            for copy in z_copies(k, c):
                copy.wait_recv()
        all_parts = [(top, total, mix), self_part]
        all_parts += [(rzs[k, 0:1, :], rzs[k, 1:2, :], rz[k].astype(F32)) for k in range(1, NZ)]
        _, whole, summed = join(all_parts)
        att[g] = (summed / whole).T.astype(BF16)
        for k in (4, 5, 3, 6, 2, 7, 1):
            gz_copy(k, ((z + k) % NZ) * 8 + g).start()

    @pl.when(z != zo)
    def _():
        gz_copy(0, c).wait_recv()

    def gx_copy(slot, target):
        return pltpu.make_async_remote_copy(
            src_ref=att.at[g], dst_ref=att.at[g], send_sem=gxs_sem.at[slot], recv_sem=gxr_sem.at[slot],
            device_id=at_ctx(target), device_id_type=MESH,
        )

    for slot in (4, 5, 2, 3, 6, 7, 1):
        gx_copy(slot, x_peer(slot // 2, slot % 2)).start()

    @pl.when(spreads_late)
    def _():
        anchor_wait()
        spread()

    @pl.when((core == 0) & (g > 0))
    def _():
        anchor_wait()
        anchor_send(5, c + 1)

    loads[6].wait()
    loads[7].wait()
    for slot in range(1, 8):
        gx_copy(slot, c).wait_recv()

    projected = nn(att[0], w_v[0:HEAD, :])
    for j in range(1, GROUPS):
        projected = projected + nn(att[j], w_v[j * HEAD : (j + 1) * HEAD, :])
    hs[...] = projected.astype(BF16).reshape(8, 16, HEAD)

    def h_copy(slot, source, target):
        return pltpu.make_async_remote_copy(
            src_ref=hs.at[source], dst_ref=hr.at[slot], send_sem=hs_sem.at[slot], recv_sem=hr_sem.at[slot],
            device_id={"ctx": c, "head": target}, device_id_type=MESH,
        )

    for slot in (6, 5, 7, 4, 2, 1, 3):
        peer = head_peer(slot // 4, slot % 4)
        h_copy(slot, peer, peer).start()

    @pl.when(core == 1)
    def _():
        anchor_wait()

    off = jnp.where(c > 0, 0.0, FAR).astype(F32)
    k_all = kk[...]
    v_all = jnp.concatenate([vv[...], jnp.ones((2 * BLOCK, HEAD), BF16)], axis=1)
    tri = lax.broadcasted_iota(jnp.int32, (ROWS, ROWS), 0) >= lax.broadcasted_iota(jnp.int32, (ROWS, ROWS), 1)
    writes = []
    for j in range(GROUPS):
        for half in range(2):
            r0 = half * ROWS
            seen = BLOCK + r0 + ROWS
            q = cq_v[r0 : r0 + ROWS, j * HEAD : (j + 1) * HEAD]
            s = nt(q, k_all[:seen]) * SCALE
            pieces = [s[:, :BLOCK] + off]
            if half:
                pieces.append(s[:, BLOCK : BLOCK + ROWS])
            pieces.append(jnp.where(tri, s[:, seen - ROWS :], FAR))
            s = jnp.concatenate(pieces, axis=1)
            m = jnp.max(s, axis=1, keepdims=True)
            p = jnp.exp(s - m).astype(BF16)
            r = nn(p, v_all[:seen])
            co_v[r0 : r0 + ROWS, j * HEAD : (j + 1) * HEAD] = (r[:, :HEAD] / r[:, HEAD:]).astype(BF16)
        if j % 2:
            cols = slice((j - 1) * HEAD, (j + 1) * HEAD)
            copy = pltpu.make_async_copy(co_v.at[:, cols], ctx_out.at[:, cols], out_sem.at[j // 2])
            copy.start()
            writes.append(copy)

    for slot in range(1, 8):
        h_copy(slot, 0, h).wait_recv()
    result = hs[h].astype(F32)
    for slot in range(1, 8):
        result = result + hr[slot].astype(F32)
    opt_out[...] = result.astype(BF16)

    for copy in writes:
        copy.wait()
    for slot in range(1, 8):
        for copy in x_copies(slot, c):
            copy.wait_send()
        gx_copy(slot, c).wait_send()
        h_copy(slot, 0, h).wait_send()

    @pl.when(z != zo)
    def _():
        for copy in z_copies(0, c):
            copy.wait_send()

    @pl.when(z == zo)
    def _():
        for k in range(1, NZ):
            gz_copy(k, c).wait_send()

    @pl.when(c == 0)
    def _():
        anchor_sent(0)
        anchor_sent(1)

    @pl.when(passes_on)
    def _():
        anchor_sent(0)

    @pl.when(g == 0)
    def _():
        for n in range(2, 6):
            anchor_sent(n)

    @pl.when((core == 0) & (g > 0))
    def _():
        anchor_sent(5)


def layer(cq, ck, cv, oq, ok, ov, seg, w):
    vmem, dma = pltpu.VMEM, pltpu.SemaphoreType.DMA
    anywhere = pl.BlockSpec(memory_space=pl.ANY)
    return pl.pallas_call(
        kernel,
        name="star_attention",
        out_shape=(
            jax.ShapeDtypeStruct((BLOCK, GROUPS * HEAD), BF16),
            jax.ShapeDtypeStruct((ROWS // 8, HEAD), BF16),
        ),
        in_specs=[anywhere] * 8,
        out_specs=(anywhere, pl.BlockSpec(memory_space=vmem)),
        scratch_shapes=[
            vmem((BLOCK, GROUPS * HEAD), BF16),
            vmem((2 * BLOCK, HEAD), BF16),
            vmem((2 * BLOCK, HEAD), BF16),
            vmem((ROWS, GROUPS * HEAD), BF16),
            vmem((ROWS, HEAD), BF16),
            vmem((ROWS, HEAD), BF16),
            vmem((1, ROWS), jnp.int32),
            vmem((GROUPS * HEAD, HEAD), BF16),
            vmem((BLOCK, GROUPS * HEAD), BF16),
            vmem((8, HEAD, ROWS), BF16),
            vmem((8, 2, ROWS), F32),
            vmem((8, HEAD, ROWS), BF16),
            vmem((8, 2, ROWS), F32),
            vmem((HEAD, ROWS), BF16),
            vmem((2, ROWS), F32),
            vmem((8, HEAD, ROWS), BF16),
            vmem((8, 2, ROWS), F32),
            vmem((8, ROWS, HEAD), BF16),
            vmem((8, 16, HEAD), BF16),
            vmem((8, 16, HEAD), BF16),
            dma((10,)),
            dma((4,)),
            dma((2, 8)),
            dma((2, 8)),
            dma((2,)),
            dma((2, 8)),
            dma((8,)),
            dma(()),
            dma((8,)),
            dma((8,)),
            dma((8,)),
            dma((8,)),
            dma((6, 2)),
            dma((2,)),
        ],
        compiler_params=pltpu.CompilerParams(collective_id=0, has_side_effects=True),
    )(cq, ck, cv, oq, ok, ov, seg.reshape(1, ROWS), w)


def solution(mesh):
    placed = (
        P("ctx", "head"),
        P("ctx", "head"),
        P("ctx", "head"),
        P(None, "head"),
        P(None, "head"),
        P(None, "head"),
        P(),
        P("head", "ctx"),
    )
    return jax.shard_map(
        layer,
        mesh=mesh,
        in_specs=placed,
        out_specs=(P("ctx", "head"), P("head", "ctx")),
        check_vma=False,
    )
```

```python
import functools

import jax
import jax.numpy as jnp
from jax import lax
from jax.experimental import pallas as pl
from jax.experimental.pallas import tpu as pltpu
from jax.sharding import PartitionSpec as P

MESH = pl.DeviceIdType.MESH
HEAD = 128
ROWS = 128
BLOCK = 256
GROUPS = 8
NZ = 8
SCALE = HEAD ** (-0.5)
FAR = -1e30
F32 = jnp.float32
BF16 = jnp.bfloat16


def nt(a, b):
    return lax.dot_general(a, b, (((1,), (1,)), ((), ())), preferred_element_type=F32)


def nn(a, b):
    return lax.dot_general(a, b, (((1,), (0,)), ((), ())), preferred_element_type=F32)


def kernel(
    cq, ck, cv, oq, ok, ov, seg, w,
    co_v, opt_out,
    cq_v, kk, vv, oq_v, ok_v, ov_v, seg_v, w_v,
    sx, sxs, rx, rxs, sz, szs, rz, rzs, att, hs, hr,
    in_sem, sx_sem, rx_sem, sz_sem, rz_sem,
    gzs_sem, gzr_sem, gxs_sem, gxr_sem, hs_sem, hr_sem, as_sem, ar_sem, near_sem,
):
    c = lax.axis_index("ctx")
    h = lax.axis_index("head")
    z, g = c // 8, c % 8
    x, core = g // 2, g % 2
    zh, y = h // 4, h % 4
    zo = 3 + core

    def at_ctx(cc):
        return {"ctx": cc, "head": h}

    def x_peer(dx, dc):
        return z * 8 + ((x + dx) % 4) * 2 + (core + dc) % 2

    def head_peer(kz, ky):
        return ((zh + kz) % 2) * 4 + (y + ky) % 4

    def along_z(k):
        zz = (zh * NZ + z + k) % (2 * NZ)
        return {"ctx": (zz % NZ) * 8 + g, "head": (zz // NZ) * 4 + y}

    def tell(sem, target):
        pl.semaphore_signal(sem, inc=1, device_id=target, device_id_type=MESH)

    own = pl.ds(BLOCK, BLOCK)
    anchor = pl.ds(0, BLOCK)
    loads = [
        pltpu.make_async_copy(ck, kk.at[own], in_sem.at[0]),
        pltpu.make_async_copy(oq, oq_v, in_sem.at[1]),
        pltpu.make_async_copy(cv, vv.at[own], in_sem.at[2]),
        pltpu.make_async_copy(ok, ok_v, in_sem.at[3]),
        pltpu.make_async_copy(ov, ov_v, in_sem.at[4]),
        pltpu.make_async_copy(seg, seg_v, in_sem.at[5]),
        pltpu.make_async_copy(w, w_v, in_sem.at[6]),
        pltpu.make_async_copy(cq, cq_v, in_sem.at[7]),
    ]
    for load in loads[:3]:
        load.start()

    barrier = pltpu.get_barrier_semaphore()
    for slot in range(1, 8):
        tell(barrier, at_ctx(x_peer(slot // 2, slot % 2)))
    for k in (1, 15):
        tell(barrier, along_z(k))
    for k in range(1, 4):
        tell(barrier, {"ctx": c, "head": head_peer(0, k)})
    for load in loads[3:]:
        load.start()
    root_loads = [
        pltpu.make_async_copy(ck, kk.at[anchor], in_sem.at[8]),
        pltpu.make_async_copy(cv, vv.at[anchor], in_sem.at[9]),
    ]

    @pl.when(c == 0)
    def _():
        for load in root_loads:
            load.start()

    def anchor_copy(i, n, target):
        ref = (kk, vv)[i]
        return pltpu.make_async_remote_copy(
            src_ref=ref.at[anchor], dst_ref=ref.at[anchor],
            send_sem=as_sem.at[n, i], recv_sem=ar_sem.at[i],
            device_id=at_ctx(target), device_id_type=MESH,
        )

    def anchor_wait(i):
        anchor_copy(i, 0, c).wait_recv()

    def anchor_sent(n):
        for i in range(2):
            anchor_copy(i, n, c).wait_send()

    def spread(i):
        for n, gg in ((2, 4), (3, 2), (4, 6), (5, 1)):
            anchor_copy(i, n, z * 8 + gg).start()

    def relay():
        for i in range(2):
            anchor_wait(i)

            @pl.when((z != 3) & (z != 7))
            def _():
                anchor_copy(i, 0, (z + 1) * 8).start()

            spread(i)

    loads[0].wait()
    loads[1].wait()
    loads[2].wait()
    k_own = kk[own, :]
    vt_own = vv[own, :].astype(F32).T.astype(BF16)

    def partial(q, keys, vt, mask=None):
        s = nt(keys, q) * SCALE
        if mask is not None:
            s = jnp.where(mask, s, FAR)
        m = jnp.max(s, axis=0, keepdims=True)
        p = jnp.exp(s - m)
        if mask is not None:
            p = jnp.where(mask, p, 0.0)
        return m, jnp.sum(p, axis=0, keepdims=True), nn(vt, p.astype(BF16))

    def x_copies(slot, target):
        return [
            pltpu.make_async_remote_copy(
                src_ref=a.at[slot], dst_ref=b.at[slot],
                send_sem=sx_sem.at[i, slot], recv_sem=rx_sem.at[i, slot],
                device_id=at_ctx(target), device_id_type=MESH,
            )
            for i, (a, b) in enumerate(((sx, rx), (sxs, rxs)))
        ]

    def option_heads(slots):
        qs = []
        for slot in slots:
            gd = ((x + slot // 2) % 4) * 2 + (core + slot % 2) % 2
            qs.append(oq_v[:, pl.ds(pl.multiple_of(gd * HEAD, HEAD), HEAD)])
        m, l, mix = partial(jnp.concatenate(qs, axis=0), k_own, vt_own)
        for n, slot in enumerate(slots):
            lanes = slice(n * ROWS, (n + 1) * ROWS)
            sx[slot] = mix[:, lanes].astype(BF16)
            sxs[slot, 0:1, :] = m[:, lanes]
            sxs[slot, 1:2, :] = l[:, lanes]

    def send_heads(slots):
        for slot in slots:
            if slot:
                for copy in x_copies(slot, x_peer(slot // 2, slot % 2)):
                    copy.start()

    option_heads((4, 5, 2, 3))
    pl.semaphore_wait(barrier, 12)
    send_heads((4, 5, 2, 3))
    for k in (1, 15):
        tell(near_sem.at[0], along_z(k))

    @pl.when(c == 0)
    def _():
        for i in range(2):
            root_loads[i].wait()
            anchor_copy(i, 1, 8).start()

    option_heads((6, 7, 1, 0))
    send_heads((6, 7, 1))
    pl.semaphore_wait(near_sem.at[0], 2)
    for k in (2, 14):
        tell(near_sem.at[1], along_z(k))

    loads[3].wait()
    loads[4].wait()
    loads[5].wait()
    seg_row = jnp.broadcast_to(seg_v[...].astype(F32), (ROWS, ROWS))
    seg_col = seg_row.T
    key_at = lax.broadcasted_iota(jnp.int32, (ROWS, ROWS), 0)
    row_at = lax.broadcasted_iota(jnp.int32, (ROWS, ROWS), 1)
    visible = (seg_row == seg_col) & (row_at >= key_at)
    q_own = oq_v[:, pl.ds(pl.multiple_of(g * HEAD, HEAD), HEAD)]
    vt_self = ov_v[...].astype(F32).T.astype(BF16)
    self_part = partial(q_own, ok_v[...], vt_self, visible)

    pl.semaphore_wait(near_sem.at[1], 2)
    for k in (4, 12):
        tell(near_sem.at[2], along_z(k))

    @pl.when(c == 0)
    def _():
        for i in range(2):
            anchor_copy(i, 0, 4 * 8).start()

    for slot in range(1, 8):
        for copy in x_copies(slot, c):
            copy.wait_recv()

    def join(parts):
        top = functools.reduce(jnp.maximum, [m for m, _, _ in parts])
        factors = [jnp.exp(m - top) for m, _, _ in parts]
        total = sum(f * l for f, (_, l, _) in zip(factors, parts))
        mix = sum(f * a for f, (_, _, a) in zip(factors, parts))
        return top, total, mix

    parts = [(sxs[0, 0:1, :], sxs[0, 1:2, :], sx[0].astype(F32))]
    parts += [(rxs[s, 0:1, :], rxs[s, 1:2, :], rx[s].astype(F32)) for s in range(1, 8)]
    top, total, mix = join(parts)

    def z_copies(k, target):
        return [
            pltpu.make_async_remote_copy(
                src_ref=a, dst_ref=b.at[k], send_sem=sz_sem.at[i], recv_sem=rz_sem.at[i, k],
                device_id=at_ctx(target), device_id_type=MESH,
            )
            for i, (a, b) in enumerate(((sz, rz), (szs, rzs)))
        ]

    def gz_copy(k, target):
        return pltpu.make_async_remote_copy(
            src_ref=att.at[g], dst_ref=att.at[g], send_sem=gzs_sem.at[k], recv_sem=gzr_sem,
            device_id=at_ctx(target), device_id_type=MESH,
        )

    @pl.when(z != zo)
    def _():
        sz[...] = mix.astype(BF16)
        szs[0:1, :] = top
        szs[1:2, :] = total
        for copy in z_copies((z - zo + NZ) % NZ, zo * 8 + g):
            copy.start()

    @pl.when((g == 0) & ((z == 1) | (z == 2) | (z == 4) | (z == 5)))
    def _():
        relay()

    @pl.when(c == 0)
    def _():
        for i in range(2):
            spread(i)

    pl.semaphore_wait(near_sem.at[2], 2)
    for k in (1, 15):
        tell(near_sem.at[3], along_z(k))

    @pl.when(z == zo)
    def _():
        for k in range(1, NZ):
            for copy in z_copies(k, c):
                copy.wait_recv()
        all_parts = [(top, total, mix), self_part]
        all_parts += [(rzs[k, 0:1, :], rzs[k, 1:2, :], rz[k].astype(F32)) for k in range(1, NZ)]
        _, whole, summed = join(all_parts)
        att[g] = (summed / whole).T.astype(BF16)
        for k in (4, 5, 3, 6, 2, 7, 1):
            gz_copy(k, ((z + k) % NZ) * 8 + g).start()

    @pl.when(z != zo)
    def _():
        gz_copy(0, c).wait_recv()

    def gx_copy(slot, target):
        return pltpu.make_async_remote_copy(
            src_ref=att.at[g], dst_ref=att.at[g], send_sem=gxs_sem.at[slot], recv_sem=gxr_sem.at[slot],
            device_id=at_ctx(target), device_id_type=MESH,
        )

    for slot in (4, 5, 2, 3, 6, 7, 1):
        gx_copy(slot, x_peer(slot // 2, slot % 2)).start()

    @pl.when((g == 0) & ((z == 3) | (z == 6)))
    def _():
        relay()

    pl.semaphore_wait(near_sem.at[3], 2)
    loads[6].wait()
    loads[7].wait()
    for slot in range(1, 8):
        gx_copy(slot, c).wait_recv()

    projected = nn(att[0], w_v[0:HEAD, :])
    for j in range(1, GROUPS):
        projected = projected + nn(att[j], w_v[j * HEAD : (j + 1) * HEAD, :])
    hs[...] = projected.astype(BF16).reshape(8, 16, HEAD)

    def h_copy(slot, source, target):
        return pltpu.make_async_remote_copy(
            src_ref=hs.at[source], dst_ref=hr.at[slot], send_sem=hs_sem.at[slot], recv_sem=hr_sem.at[slot],
            device_id={"ctx": c, "head": target}, device_id_type=MESH,
        )

    for slot in (6, 5, 7, 4, 2, 1, 3):
        peer = head_peer(slot // 4, slot % 4)
        h_copy(slot, peer, peer).start()

    @pl.when((g == 0) & (z == 7))
    def _():
        relay()

    @pl.when((core == 0) & (g > 0))
    def _():
        for i in range(2):
            anchor_wait(i)
            anchor_copy(i, 5, c + 1).start()

    @pl.when(core == 1)
    def _():
        for i in range(2):
            anchor_wait(i)

    off = jnp.where(c > 0, 0.0, FAR).astype(F32)
    k_all = kk[...]
    v_all = jnp.concatenate([vv[...], jnp.ones((2 * BLOCK, HEAD), BF16)], axis=1)
    tri = lax.broadcasted_iota(jnp.int32, (ROWS, ROWS), 0) >= lax.broadcasted_iota(jnp.int32, (ROWS, ROWS), 1)
    for j in range(GROUPS):
        for half in range(2):
            r0 = half * ROWS
            seen = BLOCK + r0 + ROWS
            q = cq_v[r0 : r0 + ROWS, j * HEAD : (j + 1) * HEAD]
            s = nt(q, k_all[:seen]) * SCALE
            pieces = [s[:, :BLOCK] + off]
            if half:
                pieces.append(s[:, BLOCK : BLOCK + ROWS])
            pieces.append(jnp.where(tri, s[:, seen - ROWS :], FAR))
            s = jnp.concatenate(pieces, axis=1)
            m = jnp.max(s, axis=1, keepdims=True)
            p = jnp.exp(s - m).astype(BF16)
            r = nn(p, v_all[:seen])
            co_v[r0 : r0 + ROWS, j * HEAD : (j + 1) * HEAD] = (r[:, :HEAD] / r[:, HEAD:]).astype(BF16)

    for slot in range(1, 8):
        h_copy(slot, 0, h).wait_recv()
    result = hs[h].astype(F32)
    for slot in range(1, 8):
        result = result + hr[slot].astype(F32)
    opt_out[...] = result.astype(BF16)

    for slot in range(1, 8):
        for copy in x_copies(slot, c):
            copy.wait_send()
        gx_copy(slot, c).wait_send()
        h_copy(slot, 0, h).wait_send()

    @pl.when(z != zo)
    def _():
        for copy in z_copies(0, c):
            copy.wait_send()

    @pl.when(z == zo)
    def _():
        for k in range(1, NZ):
            gz_copy(k, c).wait_send()

    @pl.when(c == 0)
    def _():
        anchor_sent(0)
        anchor_sent(1)

    @pl.when((g == 0) & (z > 0) & (z != 3) & (z != 7))
    def _():
        anchor_sent(0)

    @pl.when(g == 0)
    def _():
        for n in range(2, 6):
            anchor_sent(n)

    @pl.when((core == 0) & (g > 0))
    def _():
        anchor_sent(5)


def put_out(co, oo, ctx_out, opt_out, sem):
    copies = [pltpu.make_async_copy(co, ctx_out, sem.at[0]), pltpu.make_async_copy(oo, opt_out, sem.at[1])]
    for copy in copies:
        copy.start()
    for copy in copies:
        copy.wait()


def layer(cq, ck, cv, oq, ok, ov, seg, w):
    vmem, dma = pltpu.VMEM, pltpu.SemaphoreType.DMA
    anywhere = pl.BlockSpec(memory_space=pl.ANY)
    parts = pl.pallas_call(
        kernel,
        name="star_attention",
        out_shape=(vmem((BLOCK, GROUPS * HEAD), BF16), vmem((ROWS // 8, HEAD), BF16)),
        in_specs=[anywhere] * 8,
        out_specs=(pl.BlockSpec(memory_space=vmem), pl.BlockSpec(memory_space=vmem)),
        scratch_shapes=[
            vmem((BLOCK, GROUPS * HEAD), BF16),
            vmem((2 * BLOCK, HEAD), BF16),
            vmem((2 * BLOCK, HEAD), BF16),
            vmem((ROWS, GROUPS * HEAD), BF16),
            vmem((ROWS, HEAD), BF16),
            vmem((ROWS, HEAD), BF16),
            vmem((1, ROWS), jnp.int32),
            vmem((GROUPS * HEAD, HEAD), BF16),
            vmem((8, HEAD, ROWS), BF16),
            vmem((8, 2, ROWS), F32),
            vmem((8, HEAD, ROWS), BF16),
            vmem((8, 2, ROWS), F32),
            vmem((HEAD, ROWS), BF16),
            vmem((2, ROWS), F32),
            vmem((8, HEAD, ROWS), BF16),
            vmem((8, 2, ROWS), F32),
            vmem((8, ROWS, HEAD), BF16),
            vmem((8, 16, HEAD), BF16),
            vmem((8, 16, HEAD), BF16),
            dma((10,)),
            dma((2, 8)),
            dma((2, 8)),
            dma((2,)),
            dma((2, 8)),
            dma((8,)),
            dma(()),
            dma((8,)),
            dma((8,)),
            dma((8,)),
            dma((8,)),
            dma((6, 2)),
            dma((2,)),
            pltpu.SemaphoreType.REGULAR((4,)),
        ],
        compiler_params=pltpu.CompilerParams(collective_id=0, has_side_effects=True),
    )(cq, ck, cv, oq, ok, ov, seg.reshape(1, ROWS), w)
    return pl.pallas_call(
        put_out,
        name="put_out",
        out_shape=(
            jax.ShapeDtypeStruct((BLOCK, GROUPS * HEAD), BF16),
            jax.ShapeDtypeStruct((ROWS // 8, HEAD), BF16),
        ),
        in_specs=[pl.BlockSpec(memory_space=vmem)] * 2,
        out_specs=(anywhere, anywhere),
        scratch_shapes=[dma((2,))],
    )(*[pltpu.with_memory_space_constraint(part, vmem) for part in parts])


def solution(mesh):
    placed = (
        P("ctx", "head"),
        P("ctx", "head"),
        P("ctx", "head"),
        P(None, "head"),
        P(None, "head"),
        P(None, "head"),
        P(),
        P("head", "ctx"),
    )
    return jax.shard_map(
        layer,
        mesh=mesh,
        in_specs=placed,
        out_specs=(P("ctx", "head"), P("head", "ctx")),
        check_vma=False,
    )
```

```python
import functools

import jax
import jax.numpy as jnp
from jax import lax
from jax.experimental import pallas as pl
from jax.experimental.pallas import tpu as pltpu
from jax.sharding import PartitionSpec as P

MESH = pl.DeviceIdType.MESH
HEAD = 128
ROWS = 128
BLOCK = 256
GROUPS = 8
NZ = 8
OWNER_Z = 3
PIECES = 2
PIECE = HEAD // PIECES
QUARTER = BLOCK // 4
SCALE = HEAD ** (-0.5)
FAR = -1e30
F32 = jnp.float32
BF16 = jnp.bfloat16


def nt(a, b):
    return lax.dot_general(a, b, (((1,), (1,)), ((), ())), preferred_element_type=F32)


def nn(a, b):
    return lax.dot_general(a, b, (((1,), (0,)), ((), ())), preferred_element_type=F32)


def kernel(
    cq, ck, cv, oq, ok, ov, seg, w,
    ctx_out, opt_out,
    cq_v, kv, co_v, oq_v, ok_v, ov_v, seg_v, w_v, wt,
    sx, sxs, rx, rxs, sz, szs, rz, rzs, att, hs, hr,
    in_sem, out_sem, sx_sem, rx_sem, sz_sem, rz_sem,
    gzs_sem, gzr_sem, gxs_sem, gxr_sem, hs_sem, hr_sem, as_sem, ar_sem, near_sem,
):
    c = lax.axis_index("ctx")
    h = lax.axis_index("head")
    z, g = c // 8, c % 8
    x, core = g // 2, g % 2
    zh, y = h // 4, h % 4
    zo = OWNER_Z + core

    def at_ctx(cc):
        return {"ctx": cc, "head": h}

    def x_peer(dx, dc):
        return z * 8 + ((x + dx) % 4) * 2 + (core + dc) % 2

    def head_peer(kz, ky):
        return ((zh + kz) % 2) * 4 + (y + ky) % 4

    def along_z(k):
        zz = (zh * NZ + z + k) % (2 * NZ)
        return {"ctx": (zz % NZ) * 8 + g, "head": (zz // NZ) * 4 + y}

    def tell(sem, target):
        pl.semaphore_signal(sem, inc=1, device_id=target, device_id_type=MESH)

    own = pl.ds(BLOCK, BLOCK)
    anchor = pl.ds(0, BLOCK)
    def arrived(ref, sem):
        pltpu.make_async_copy(ref, ref, sem).wait()

    def query_load(dx):
        cols = pl.ds(pl.multiple_of(((x + dx) % 4) * 2 * HEAD, 2 * HEAD), 2 * HEAD)
        return pltpu.make_async_copy(oq.at[:, cols], oq_v.at[:, cols], in_sem.at[0 if dx in (1, 2) else 1])

    pltpu.make_async_copy(ck, kv.at[0, own], in_sem.at[0]).start()
    for dx in (2, 1):
        query_load(dx).start()
    pltpu.make_async_copy(cv, kv.at[1, own], in_sem.at[0]).start()
    for dx in (3, 0):
        query_load(dx).start()

    barrier = pltpu.get_barrier_semaphore()
    for slot in range(1, 8):
        tell(barrier, at_ctx(x_peer(slot // 2, slot % 2)))
    for k in (1, 15):
        tell(barrier, along_z(k))
    for k in range(1, 4):
        tell(barrier, {"ctx": c, "head": head_peer(0, k)})
    pltpu.make_async_copy(ok, ok_v, in_sem.at[2]).start()
    pltpu.make_async_copy(ov, ov_v, in_sem.at[2]).start()
    pltpu.make_async_copy(seg, seg_v, in_sem.at[3]).start()
    pltpu.make_async_copy(w, w_v, in_sem.at[4]).start()
    pltpu.make_async_copy(cq, cq_v, in_sem.at[5]).start()

    @pl.when(c == 0)
    def _():
        pltpu.make_async_copy(ck, kv.at[0, anchor], in_sem.at[6]).start()
        pltpu.make_async_copy(cv, kv.at[1, anchor], in_sem.at[6]).start()

    def anchor_copy(q, n, target):
        ref = kv.at[:, pl.ds(pl.multiple_of(q * QUARTER, QUARTER), QUARTER)]
        return pltpu.make_async_remote_copy(
            src_ref=ref, dst_ref=ref, send_sem=as_sem.at[n], recv_sem=ar_sem.at[q],
            device_id=at_ctx(target), device_id_type=MESH,
        )

    def anchor_sent(n, quarters):
        arrived(kv.at[:, 0 : quarters * QUARTER], as_sem.at[n])

    arrived(oq_v, in_sem.at[0])
    k_own = kv[0, own, :]
    vt_own = kv[1, own, :].astype(F32).T.astype(BF16)

    def partial(q, keys, vt, mask=None):
        s = nt(keys, q) * SCALE
        if mask is not None:
            s = jnp.where(mask, s, FAR)
        m = jnp.max(s, axis=0, keepdims=True)
        p = jnp.exp(s - m)
        if mask is not None:
            p = jnp.where(mask, p, 0.0)
        return m, jnp.sum(p, axis=0, keepdims=True), nn(vt, p.astype(BF16))

    def x_copy(i, slot, target):
        src, dst = (sxs, rxs) if i == PIECES else (sx.at[i], rx.at[i])
        return pltpu.make_async_remote_copy(
            src_ref=src.at[slot], dst_ref=dst.at[slot],
            send_sem=sx_sem.at[i], recv_sem=rx_sem.at[i],
            device_id=at_ctx(target), device_id_type=MESH,
        )

    others = pl.ds(1, 7)

    def piece(i):
        return slice(i * PIECE, (i + 1) * PIECE)

    def option_heads(slots):
        qs = []
        for slot in slots:
            gd = ((x + slot // 2) % 4) * 2 + (core + slot % 2) % 2
            qs.append(oq_v[:, pl.ds(pl.multiple_of(gd * HEAD, HEAD), HEAD)])
        m, l, mix = partial(jnp.concatenate(qs, axis=0), k_own, vt_own)
        for n, slot in enumerate(slots):
            lanes = slice(n * ROWS, (n + 1) * ROWS)
            for i in range(PIECES):
                sx[i, slot] = mix[piece(i), lanes].astype(BF16)
            sxs[slot, 0:1, :] = m[:, lanes]
            sxs[slot, 1:2, :] = l[:, lanes]

    def send_heads(i, slots):
        for slot in slots:
            x_copy(i, slot, x_peer(slot // 2, slot % 2)).start()

    option_heads((4, 5, 2, 3))
    pl.semaphore_wait(barrier, 12)
    send_heads(PIECES, (4, 5, 2, 3))
    send_heads(0, (4, 5, 2, 3))
    for k in (1, 15):
        tell(near_sem.at[0], along_z(k))

    arrived(oq_v.at[:, 0 : 4 * HEAD], in_sem.at[1])
    option_heads((6, 7, 1, 0))
    send_heads(PIECES, (6, 7, 1))
    send_heads(0, (6, 7, 1))
    for i in range(1, PIECES):
        send_heads(i, (4, 5, 2, 3, 6, 7, 1))

    @pl.when(c == 0)
    def _():
        arrived(kv.at[:, anchor], in_sem.at[6])
        for q in (2, 1, 3):
            anchor_copy(q, 0, q * 2).start()

    pl.semaphore_wait(near_sem.at[0], 2)
    for k in (2, 14):
        tell(near_sem.at[1], along_z(k))

    arrived(kv.at[0, own], in_sem.at[2])
    arrived(seg_v, in_sem.at[3])
    seg_row = jnp.broadcast_to(seg_v[...].astype(F32), (ROWS, ROWS))
    seg_col = seg_row.T
    key_at = lax.broadcasted_iota(jnp.int32, (ROWS, ROWS), 0)
    row_at = lax.broadcasted_iota(jnp.int32, (ROWS, ROWS), 1)
    visible = (seg_row == seg_col) & (row_at >= key_at)
    q_own = oq_v[:, pl.ds(pl.multiple_of(g * HEAD, HEAD), HEAD)]
    vt_self = ov_v[...].astype(F32).T.astype(BF16)
    self_part = partial(q_own, ok_v[...], vt_self, visible)

    arrived(w_v, in_sem.at[4])
    for i in range(PIECES):
        rows = [w_v[j * HEAD + i * PIECE : j * HEAD + (i + 1) * PIECE, :] for j in range(GROUPS)]
        wt[i] = jnp.concatenate(rows, axis=0).astype(F32).T.astype(BF16)

    pl.semaphore_wait(near_sem.at[1], 2)
    for k in (4, 12):
        tell(near_sem.at[2], along_z(k))

    def factors_of(tops):
        top = functools.reduce(jnp.maximum, tops)
        return top, [jnp.exp(m - top) for m in tops]

    def z_copy(i, k, target):
        src, dst = (szs, rzs) if i == PIECES else (sz.at[i], rz.at[i])
        return pltpu.make_async_remote_copy(
            src_ref=src, dst_ref=dst.at[k], send_sem=sz_sem.at[i], recv_sem=rz_sem.at[i],
            device_id=at_ctx(target), device_id_type=MESH,
        )

    to_owner = (z - zo + NZ) % NZ
    owner = zo * 8 + g
    arrived(rxs.at[others], rx_sem.at[PIECES])
    top, factors = factors_of([sxs[0, 0:1, :]] + [rxs[k, 0:1, :] for k in range(1, 8)])
    total = factors[0] * sxs[0, 1:2, :]
    for k in range(1, 8):
        total = total + factors[k] * rxs[k, 1:2, :]

    @pl.when(z != zo)
    def _():
        szs[0:1, :] = top
        szs[1:2, :] = total
        z_copy(PIECES, to_owner, owner).start()

    mixes = []
    for i in range(PIECES):
        arrived(rx.at[i, others], rx_sem.at[i])
        mix = factors[0] * sx[i, 0].astype(F32)
        for k in range(1, 8):
            mix = mix + factors[k] * rx[i, k].astype(F32)
        mixes.append(mix)

        @pl.when(z != zo)
        def _():
            sz[i] = mix.astype(BF16)
            z_copy(i, to_owner, owner).start()

    at_foot = (z == 0) & (core == 0)

    def anchor_up():
        @pl.when(x > 0)
        def _():
            anchor_copy(x, 0, c).wait_recv()

        for k in (7, 6, 5, 4, 3, 2, 1):
            anchor_copy(x, 1, k * 8 + g).start()

    pl.semaphore_wait(near_sem.at[2], 2)
    for k in (1, 15):
        tell(near_sem.at[3], along_z(k))

    @pl.when(at_foot)
    def _():
        anchor_up()

    def gz_copy(i, target):
        return pltpu.make_async_remote_copy(
            src_ref=att.at[i, g], dst_ref=att.at[i, g], send_sem=gzs_sem.at[i], recv_sem=gzr_sem.at[i],
            device_id=at_ctx(target), device_id_type=MESH,
        )

    def gx_copy(i, target):
        return pltpu.make_async_remote_copy(
            src_ref=att.at[i, g], dst_ref=att.at[i, g], send_sem=gxs_sem.at[i], recv_sem=gxr_sem.at[i],
            device_id=at_ctx(target), device_id_type=MESH,
        )

    def gx_send(i):
        for slot in (4, 5, 2, 3, 6, 7, 1):
            gx_copy(i, x_peer(slot // 2, slot % 2)).start()

    @pl.when(z == zo)
    def _():
        self_top, self_total, self_mix = self_part
        arrived(rzs.at[others], rz_sem.at[PIECES])
        _, parts = factors_of([top, self_top] + [rzs[k, 0:1, :] for k in range(1, NZ)])
        whole = parts[0] * total + parts[1] * self_total
        for k in range(1, NZ):
            whole = whole + parts[k + 1] * rzs[k, 1:2, :]
        for i in range(PIECES):
            arrived(rz.at[i, others], rz_sem.at[i])
            summed = parts[0] * mixes[i] + parts[1] * self_mix[piece(i)]
            for k in range(1, NZ):
                summed = summed + parts[k + 1] * rz[i, k].astype(F32)
            att[i, g] = (summed / whole).astype(BF16)
            for k in (5, 4, 6, 7, 1, 2, 3):
                gz_copy(i, ((z + k) % NZ) * 8 + g).start()
        for i in range(PIECES):
            gx_send(i)

    @pl.when(z != zo)
    def _():
        for i in range(PIECES):
            arrived(att.at[i, 0], gzr_sem.at[i])
            gx_send(i)

    pl.semaphore_wait(near_sem.at[3], 2)
    arrived(cq_v, in_sem.at[5])

    projected = None
    for i in range(PIECES):
        arrived(att.at[i, others], gxr_sem.at[i])
        share = nn(wt[i], att[i].reshape(GROUPS * PIECE, ROWS))
        projected = share if projected is None else projected + share
    hs[...] = projected.T.astype(BF16).reshape(8, 16, HEAD)

    def h_copy(slot, source, target):
        return pltpu.make_async_remote_copy(
            src_ref=hs.at[source], dst_ref=hr.at[slot], send_sem=hs_sem, recv_sem=hr_sem,
            device_id={"ctx": c, "head": target}, device_id_type=MESH,
        )

    for slot in (6, 5, 7, 4, 2, 1, 3):
        peer = head_peer(slot // 4, slot % 4)
        h_copy(slot, peer, peer).start()

    @pl.when(core == 0)
    def _():
        @pl.when(z > 0)
        def _():
            anchor_copy(x, 0, c).wait_recv()

        for k in (2, 1, 3):

            @pl.when((z > 0) | ((x + k) % 4 > 0))
            def _():
                anchor_copy(x, 2, z * 8 + ((x + k) % 4) * 2).start()

        anchor_copy(x, 3, c + 1).start()

    @pl.when((core == 0) & (c > 0))
    def _():
        for k in (1, 3, 2):
            q = (x + k) % 4
            anchor_copy(q, 0, c).wait_recv()
            anchor_copy(q, 3, c + 1).start()

    @pl.when(c == 0)
    def _():
        for q in range(1, 4):
            anchor_copy(q, 3, 1).start()

    @pl.when(core == 1)
    def _():
        for q in range(4):
            anchor_copy(q, 0, c).wait_recv()

    off = jnp.where(c > 0, 0.0, FAR).astype(F32)
    k_all = kv[0]
    v_all = jnp.concatenate([kv[1], jnp.ones((2 * BLOCK, HEAD), BF16)], axis=1)
    tri = lax.broadcasted_iota(jnp.int32, (ROWS, ROWS), 0) >= lax.broadcasted_iota(jnp.int32, (ROWS, ROWS), 1)
    for j in range(GROUPS):
        for half in range(2):
            r0 = half * ROWS
            seen = BLOCK + r0 + ROWS
            q = cq_v[r0 : r0 + ROWS, j * HEAD : (j + 1) * HEAD]
            s = nt(q, k_all[:seen]) * SCALE
            pieces = [s[:, :BLOCK] + off]
            if half:
                pieces.append(s[:, BLOCK : BLOCK + ROWS])
            pieces.append(jnp.where(tri, s[:, seen - ROWS :], FAR))
            s = jnp.concatenate(pieces, axis=1)
            m = jnp.max(s, axis=1, keepdims=True)
            p = jnp.exp(s - m).astype(BF16)
            r = nn(p, v_all[:seen])
            co_v[r0 : r0 + ROWS, j * HEAD : (j + 1) * HEAD] = (r[:, :HEAD] / r[:, HEAD:]).astype(BF16)
        if j % 2:
            cols = slice((j - 1) * HEAD, (j + 1) * HEAD)
            pltpu.make_async_copy(co_v.at[:, cols], ctx_out.at[:, cols], out_sem).start()

    arrived(co_v, out_sem)
    arrived(sxs.at[others], sx_sem.at[PIECES])
    arrived(hs.at[others], hs_sem)
    for i in range(PIECES):
        arrived(sx.at[i, others], sx_sem.at[i])
        arrived(att.at[i, others], gxs_sem.at[i])

    @pl.when(z != zo)
    def _():
        arrived(szs, sz_sem.at[PIECES])
        for i in range(PIECES):
            arrived(sz.at[i], sz_sem.at[i])

    @pl.when(z == zo)
    def _():
        for i in range(PIECES):
            arrived(att.at[i, others], gzs_sem.at[i])

    @pl.when(c == 0)
    def _():
        anchor_sent(0, 3)

    @pl.when(at_foot)
    def _():
        anchor_sent(1, 7)

    @pl.when(core == 0)
    def _():
        @pl.when((z == 0) & (x > 0))
        def _():
            anchor_sent(2, 2)

        @pl.when((z > 0) | (x == 0))
        def _():
            anchor_sent(2, 3)

        anchor_sent(3, 4)

    arrived(hr.at[others], hr_sem)
    result = hs[h].astype(F32)
    for slot in range(1, 8):
        result = result + hr[slot].astype(F32)
    opt_out[...] = result.astype(BF16)


def put_out(co, oo, ctx_out, opt_out, sem):
    copies = [pltpu.make_async_copy(oo, opt_out, sem.at[8])]
    for n in range(8):
        rows = pl.ds(n * 32, 32)
        copies.append(pltpu.make_async_copy(co.at[rows], ctx_out.at[rows], sem.at[n]))
    for copy in copies:
        copy.start()
    for copy in copies:
        copy.wait()


def layer(cq, ck, cv, oq, ok, ov, seg, w):
    vmem, dma = pltpu.VMEM, pltpu.SemaphoreType.DMA
    anywhere = pl.BlockSpec(memory_space=pl.ANY)
    parts = pl.pallas_call(
        kernel,
        name="star_attention",
        out_shape=(vmem((BLOCK, GROUPS * HEAD), BF16), vmem((ROWS // 8, HEAD), BF16)),
        in_specs=[anywhere] * 8,
        out_specs=(anywhere, pl.BlockSpec(memory_space=vmem)),
        scratch_shapes=[
            vmem((BLOCK, GROUPS * HEAD), BF16),
            vmem((2, 2 * BLOCK, HEAD), BF16),
            vmem((BLOCK, GROUPS * HEAD), BF16),
            vmem((ROWS, GROUPS * HEAD), BF16),
            vmem((ROWS, HEAD), BF16),
            vmem((ROWS, HEAD), BF16),
            vmem((1, ROWS), jnp.int32),
            vmem((GROUPS * HEAD, HEAD), BF16),
            vmem((PIECES, HEAD, GROUPS * PIECE), BF16),
            vmem((PIECES, 8, PIECE, ROWS), BF16),
            vmem((8, 2, ROWS), F32),
            vmem((PIECES, 8, PIECE, ROWS), BF16),
            vmem((8, 2, ROWS), F32),
            vmem((PIECES, PIECE, ROWS), BF16),
            vmem((2, ROWS), F32),
            vmem((PIECES, 8, PIECE, ROWS), BF16),
            vmem((8, 2, ROWS), F32),
            vmem((PIECES, 8, PIECE, ROWS), BF16),
            vmem((8, 16, HEAD), BF16),
            vmem((8, 16, HEAD), BF16),
            dma((7,)),
            dma(()),
            dma((PIECES + 1,)),
            dma((PIECES + 1,)),
            dma((PIECES + 1,)),
            dma((PIECES + 1,)),
            dma((PIECES,)),
            dma((PIECES,)),
            dma((PIECES,)),
            dma((PIECES,)),
            dma(()),
            dma(()),
            dma((4,)),
            dma((4,)),
            pltpu.SemaphoreType.REGULAR((4,)),
        ],
        compiler_params=pltpu.CompilerParams(collective_id=0, has_side_effects=True),
    )(cq, ck, cv, oq, ok, ov, seg.reshape(1, ROWS), w)
    return pl.pallas_call(
        put_out,
        name="put_out",
        out_shape=(
            jax.ShapeDtypeStruct((BLOCK, GROUPS * HEAD), BF16),
            jax.ShapeDtypeStruct((ROWS // 8, HEAD), BF16),
        ),
        in_specs=[pl.BlockSpec(memory_space=vmem)] * 2,
        out_specs=(anywhere, anywhere),
        scratch_shapes=[dma((9,))],
    )(*[pltpu.with_memory_space_constraint(part, vmem) for part in parts])


def solution(mesh):
    placed = (
        P("ctx", "head"),
        P("ctx", "head"),
        P("ctx", "head"),
        P(None, "head"),
        P(None, "head"),
        P(None, "head"),
        P(),
        P("head", "ctx"),
    )
    return jax.shard_map(
        layer,
        mesh=mesh,
        in_specs=placed,
        out_specs=(P("ctx", "head"), P("head", "ctx")),
        check_vma=False,
    )
```

```python
import functools

import jax
import jax.numpy as jnp
from jax import lax
from jax.experimental import pallas as pl
from jax.experimental.pallas import tpu as pltpu
from jax.sharding import PartitionSpec as P

MESH = pl.DeviceIdType.MESH
HEAD = 128
ROWS = 128
BLOCK = 256
GROUPS = 8
NZ = 8
OWNER_Z = 3
PIECES = 2
PIECE = HEAD // PIECES
QUARTER = BLOCK // 4
SCALE = HEAD ** (-0.5)
FAR = -1e30
F32 = jnp.float32
BF16 = jnp.bfloat16


def nt(a, b):
    return lax.dot_general(a, b, (((1,), (1,)), ((), ())), preferred_element_type=F32)


def nn(a, b):
    return lax.dot_general(a, b, (((1,), (0,)), ((), ())), preferred_element_type=F32)


def kernel(
    cq, ck, cv, oq, ok, ov, seg, w,
    ctx_out, opt_out,
    cq_v, kv, co_v, oq_v, ok_v, ov_v, seg_v, w_v, wt,
    sx, sxs, px, pxs, rx, rxs, sz, szs, rz, rzs, owned, att, hs, hr,
    in_sem, out_sem, sp_sem, rp_sem, sx_sem, rx_sem, sz_sem, rz_sem,
    gzs_sem, gzr_sem, gxs_sem, gxr_sem, hs_sem, hr_sem, as_sem, ar_sem, near_sem, pair_sem,
):
    c = lax.axis_index("ctx")
    h = lax.axis_index("head")
    z, g = c // 8, c % 8
    x, core = g // 2, g % 2
    zh, y = h // 4, h % 4
    zo = OWNER_Z + core
    owner = zo * 8 + x * 2 + 1
    partner = z * 8 + x * 2 + (core + 1) % 2
    owns_even = (core == 1) & (z == OWNER_Z)
    owns_odd = (core == 1) & (z == OWNER_Z + 1)
    owned_head = x * 2 + (z + OWNER_Z) % 2

    def at_ctx(cc):
        return {"ctx": cc, "head": h}

    def x_peer(dx, dc):
        return z * 8 + ((x + dx) % 4) * 2 + (core + dc) % 2

    def head_peer(kz, ky):
        return ((zh + kz) % 2) * 4 + (y + ky) % 4

    def along_z(k):
        zz = (zh * NZ + z + k) % (2 * NZ)
        return {"ctx": (zz % NZ) * 8 + g, "head": (zz // NZ) * 4 + y}

    def tell(sem, target):
        pl.semaphore_signal(sem, inc=1, device_id=target, device_id_type=MESH)

    own = pl.ds(BLOCK, BLOCK)
    anchor = pl.ds(0, BLOCK)
    def arrived(ref, sem):
        pltpu.make_async_copy(ref, ref, sem).wait()

    def query_load(dx):
        cols = pl.ds(pl.multiple_of(((x + dx) % 4) * 2 * HEAD, 2 * HEAD), 2 * HEAD)
        return pltpu.make_async_copy(oq.at[:, cols], oq_v.at[:, cols], in_sem.at[0 if dx in (1, 2) else 1])

    pltpu.make_async_copy(ck, kv.at[0, own], in_sem.at[0]).start()
    for dx in (2, 1):
        query_load(dx).start()
    pltpu.make_async_copy(cv, kv.at[1, own], in_sem.at[0]).start()
    for dx in (3, 0):
        query_load(dx).start()

    barrier = pltpu.get_barrier_semaphore()
    for slot in range(1, 8):
        tell(barrier, at_ctx(x_peer(slot // 2, slot % 2)))
    for k in (1, 15):
        tell(barrier, along_z(k))
    for k in range(1, 4):
        tell(barrier, {"ctx": c, "head": head_peer(0, k)})
    pltpu.make_async_copy(ok, ok_v, in_sem.at[2]).start()
    pltpu.make_async_copy(ov, ov_v, in_sem.at[2]).start()
    pltpu.make_async_copy(seg, seg_v, in_sem.at[3]).start()
    pltpu.make_async_copy(w, w_v, in_sem.at[4]).start()
    pltpu.make_async_copy(cq, cq_v, in_sem.at[5]).start()

    @pl.when(c == 0)
    def _():
        pltpu.make_async_copy(ck, kv.at[0, anchor], in_sem.at[6]).start()
        pltpu.make_async_copy(cv, kv.at[1, anchor], in_sem.at[6]).start()

    def anchor_copy(q, n, target):
        ref = kv.at[:, pl.ds(pl.multiple_of(q * QUARTER, QUARTER), QUARTER)]
        return pltpu.make_async_remote_copy(
            src_ref=ref, dst_ref=ref, send_sem=as_sem.at[n], recv_sem=ar_sem.at[q],
            device_id=at_ctx(target), device_id_type=MESH,
        )

    def anchor_sent(n, quarters):
        arrived(kv.at[:, 0 : quarters * QUARTER], as_sem.at[n])

    arrived(oq_v, in_sem.at[0])
    k_own = kv[0, own, :]
    vt_own = kv[1, own, :].astype(F32).T.astype(BF16)

    def partial(q, keys, vt, mask=None):
        s = nt(keys, q) * SCALE
        if mask is not None:
            s = jnp.where(mask, s, FAR)
        m = jnp.max(s, axis=0, keepdims=True)
        p = jnp.exp(s - m)
        if mask is not None:
            p = jnp.where(mask, p, 0.0)
        return m, jnp.sum(p, axis=0, keepdims=True), nn(vt, p.astype(BF16))

    def x_copy(i, slot, target):
        src, dst = (sxs, rxs) if i == PIECES else (sx.at[i], rx.at[i])
        return pltpu.make_async_remote_copy(
            src_ref=src.at[slot], dst_ref=dst.at[slot],
            send_sem=sx_sem.at[i], recv_sem=rx_sem.at[i],
            device_id=at_ctx(target), device_id_type=MESH,
        )

    others = pl.ds(1, 7)
    six = pl.ds(1, 6)
    senders = (1, 2, 3, 4, 6, 7)

    def piece(i):
        return slice(i * PIECE, (i + 1) * PIECE)

    def option_heads(slots):
        qs = []
        for slot in slots:
            gd = ((x + slot // 2) % 4) * 2 + (core + slot % 2) % 2
            qs.append(oq_v[:, pl.ds(pl.multiple_of(gd * HEAD, HEAD), HEAD)])
        m, l, mix = partial(jnp.concatenate(qs, axis=0), k_own, vt_own)
        for n, slot in enumerate(slots):
            lanes = slice(n * ROWS, (n + 1) * ROWS)
            for i in range(PIECES):
                sx[i, slot] = mix[piece(i), lanes].astype(BF16)
            sxs[slot, 0:1, :] = m[:, lanes]
            sxs[slot, 1:2, :] = l[:, lanes]

    def send_heads(i, slots):
        for slot in slots:
            x_copy(i, slot, x_peer(slot // 2, slot % 2)).start()

    def pair_copy(i):
        src, dst = (sxs, pxs) if i == PIECES else (sx.at[i], px.at[i])
        return pltpu.make_async_remote_copy(
            src_ref=src.at[5], dst_ref=dst, send_sem=sp_sem.at[i], recv_sem=rp_sem.at[i],
            device_id=at_ctx(partner), device_id_type=MESH,
        )

    option_heads((5, 4))
    pl.semaphore_wait(barrier, 12)
    for i in (PIECES, *range(PIECES)):
        pair_copy(i).start()
    for k in (1, 15):
        tell(near_sem.at[0], along_z(k))

    arrived(oq_v.at[:, 0 : 4 * HEAD], in_sem.at[1])
    option_heads((2, 3, 6, 7))
    send_heads(PIECES, (2, 3, 6, 7))
    send_heads(0, (2, 3, 6, 7))

    arrived(pxs, rp_sem.at[PIECES])
    m_here, m_there = sxs[4, 0:1, :], pxs[0:1, :]
    m_pair = jnp.maximum(m_here, m_there)
    f_here, f_there = jnp.exp(m_here - m_pair), jnp.exp(m_there - m_pair)
    l_pair = f_here * sxs[4, 1:2, :] + f_there * pxs[1:2, :]
    sxs[4, 0:1, :] = m_pair
    sxs[4, 1:2, :] = l_pair
    for i in range(PIECES):
        arrived(px.at[i], rp_sem.at[i])
        sx[i, 4] = (f_here * sx[i, 4].astype(F32) + f_there * px[i].astype(F32)).astype(BF16)
    send_heads(PIECES, (4,))
    for i in range(PIECES):
        send_heads(i, (4,))
    option_heads((1, 0))
    send_heads(PIECES, (1,))
    send_heads(0, (1,))
    for i in range(1, PIECES):
        send_heads(i, (2, 3, 6, 7, 1))

    @pl.when(c == 0)
    def _():
        arrived(kv.at[:, anchor], in_sem.at[6])
        for q in (2, 1, 3):
            anchor_copy(q, 0, q * 2).start()

    pl.semaphore_wait(near_sem.at[0], 2)
    for k in (2, 14):
        tell(near_sem.at[1], along_z(k))

    arrived(kv.at[0, own], in_sem.at[2])
    arrived(seg_v, in_sem.at[3])
    seg_row = jnp.broadcast_to(seg_v[...].astype(F32), (ROWS, ROWS))
    seg_col = seg_row.T
    key_at = lax.broadcasted_iota(jnp.int32, (ROWS, ROWS), 0)
    row_at = lax.broadcasted_iota(jnp.int32, (ROWS, ROWS), 1)
    visible = (seg_row == seg_col) & (row_at >= key_at)
    q_own = oq_v[:, pl.ds(pl.multiple_of(owned_head * HEAD, HEAD), HEAD)]
    vt_self = ov_v[...].astype(F32).T.astype(BF16)
    self_part = partial(q_own, ok_v[...], vt_self, visible)

    arrived(w_v, in_sem.at[4])
    for i in range(PIECES):
        rows = [w_v[j * HEAD + i * PIECE : j * HEAD + (i + 1) * PIECE, :] for j in range(GROUPS)]
        wt[i] = jnp.concatenate(rows, axis=0).astype(F32).T.astype(BF16)

    pl.semaphore_wait(near_sem.at[1], 2)
    for k in (4, 12):
        tell(near_sem.at[2], along_z(k))

    @pl.when(core == 1)
    def _():
        tell(pair_sem, at_ctx(partner))

    def factors_of(tops):
        top = functools.reduce(jnp.maximum, tops)
        return top, [jnp.exp(m - top) for m in tops]

    def z_copy(i, k, target):
        src, dst = (szs, rzs) if i == PIECES else (sz.at[i], rz.at[i])
        return pltpu.make_async_remote_copy(
            src_ref=src, dst_ref=dst.at[k], send_sem=sz_sem.at[i], recv_sem=rz_sem.at[i],
            device_id=at_ctx(target), device_id_type=MESH,
        )

    arrived(rxs.at[six], rx_sem.at[PIECES])
    top, factors = factors_of([sxs[0, 0:1, :]] + [rxs[k, 0:1, :] for k in senders])
    total = factors[0] * sxs[0, 1:2, :]
    for n, k in enumerate(senders):
        total = total + factors[n + 1] * rxs[k, 1:2, :]

    @pl.when(core == 0)
    def _():
        pl.semaphore_wait(pair_sem, 1)

    @pl.when(~owns_odd)
    def _():
        szs[0:1, :] = top
        szs[1:2, :] = total
        z_copy(PIECES, z, owner).start()

    @pl.when(owns_odd)
    def _():
        rzs[OWNER_Z + 1, 0:1, :] = top
        rzs[OWNER_Z + 1, 1:2, :] = total

    for i in range(PIECES):
        arrived(rx.at[i, six], rx_sem.at[i])
        mix = factors[0] * sx[i, 0].astype(F32)
        for n, k in enumerate(senders):
            mix = mix + factors[n + 1] * rx[i, k].astype(F32)

        @pl.when(~owns_odd)
        def _():
            sz[i] = mix.astype(BF16)
            z_copy(i, z, owner).start()

        @pl.when(owns_odd)
        def _():
            rz[i, OWNER_Z + 1] = mix.astype(BF16)

    at_foot = (z == 0) & (core == 0)

    def anchor_up():
        @pl.when(x > 0)
        def _():
            anchor_copy(x, 0, c).wait_recv()

        for k in (7, 6, 5, 4, 3, 2, 1):
            anchor_copy(x, 1, k * 8 + g).start()

    pl.semaphore_wait(near_sem.at[2], 2)
    for k in (1, 15):
        tell(near_sem.at[3], along_z(k))

    @pl.when(at_foot)
    def _():
        anchor_up()

    def gz_copy(i, target):
        return pltpu.make_async_remote_copy(
            src_ref=owned.at[i], dst_ref=att.at[i, owned_head], send_sem=gzs_sem.at[i], recv_sem=gzr_sem.at[i],
            device_id=at_ctx(target), device_id_type=MESH,
        )

    def gx_copy(i, target):
        return pltpu.make_async_remote_copy(
            src_ref=att.at[i, g], dst_ref=att.at[i, g], send_sem=gxs_sem.at[i], recv_sem=gxr_sem.at[i],
            device_id=at_ctx(target), device_id_type=MESH,
        )

    def gx_send(i):
        for slot in (4, 5, 2, 3, 6, 7, 1):
            gx_copy(i, x_peer(slot // 2, slot % 2)).start()

    def column_arrived(ref, sem):
        @pl.when(owns_even)
        def _():
            arrived(ref, sem)

        @pl.when(owns_odd)
        def _():
            arrived(ref.at[others], sem)

    @pl.when(owns_even | owns_odd)
    def _():
        self_top, self_total, self_mix = self_part
        column_arrived(rzs, rz_sem.at[PIECES])
        _, parts = factors_of([self_top] + [rzs[k, 0:1, :] for k in range(NZ)])
        whole = parts[0] * self_total
        for k in range(NZ):
            whole = whole + parts[k + 1] * rzs[k, 1:2, :]
        for i in range(PIECES):
            column_arrived(rz.at[i], rz_sem.at[i])
            summed = parts[0] * self_mix[piece(i)]
            for k in range(NZ):
                summed = summed + parts[k + 1] * rz[i, k].astype(F32)
            owned[i] = (summed / whole).astype(BF16)

            @pl.when(owns_odd)
            def _():
                att[i, g] = owned[i]

            for k in (0, 1, 2, 7, 3, 6, 5):
                gz_copy(i, k * 8 + owned_head).start()

            @pl.when(owns_even)
            def _():
                gz_copy(i, 4 * 8 + owned_head).start()

    @pl.when(owns_odd)
    def _():
        for i in range(PIECES):
            gx_send(i)

    @pl.when(~owns_odd)
    def _():
        for i in range(PIECES):
            arrived(att.at[i, 0], gzr_sem.at[i])
            gx_send(i)

    pl.semaphore_wait(near_sem.at[3], 2)
    arrived(cq_v, in_sem.at[5])

    projected = None
    for i in range(PIECES):
        arrived(att.at[i, others], gxr_sem.at[i])
        share = nn(wt[i], att[i].reshape(GROUPS * PIECE, ROWS))
        projected = share if projected is None else projected + share
    hs[...] = projected.T.astype(BF16).reshape(8, 16, HEAD)

    def h_copy(slot, source, target):
        return pltpu.make_async_remote_copy(
            src_ref=hs.at[source], dst_ref=hr.at[slot], send_sem=hs_sem, recv_sem=hr_sem,
            device_id={"ctx": c, "head": target}, device_id_type=MESH,
        )

    for slot in (6, 5, 7, 4, 2, 1, 3):
        peer = head_peer(slot // 4, slot % 4)
        h_copy(slot, peer, peer).start()

    @pl.when(core == 0)
    def _():
        @pl.when(z > 0)
        def _():
            anchor_copy(x, 0, c).wait_recv()

        for k in (2, 1, 3):

            @pl.when((z > 0) | ((x + k) % 4 > 0))
            def _():
                anchor_copy(x, 2, z * 8 + ((x + k) % 4) * 2).start()

        anchor_copy(x, 3, c + 1).start()

    @pl.when((core == 0) & (c > 0))
    def _():
        for k in (1, 3, 2):
            q = (x + k) % 4
            anchor_copy(q, 0, c).wait_recv()
            anchor_copy(q, 3, c + 1).start()

    @pl.when(c == 0)
    def _():
        for q in range(1, 4):
            anchor_copy(q, 3, 1).start()

    @pl.when(core == 1)
    def _():
        for q in range(4):
            anchor_copy(q, 0, c).wait_recv()

    off = jnp.where(c > 0, 0.0, FAR).astype(F32)
    k_all = kv[0]
    v_all = jnp.concatenate([kv[1], jnp.ones((2 * BLOCK, HEAD), BF16)], axis=1)
    tri = lax.broadcasted_iota(jnp.int32, (ROWS, ROWS), 0) >= lax.broadcasted_iota(jnp.int32, (ROWS, ROWS), 1)
    for j in range(GROUPS):
        for half in range(2):
            r0 = half * ROWS
            seen = BLOCK + r0 + ROWS
            q = cq_v[r0 : r0 + ROWS, j * HEAD : (j + 1) * HEAD]
            s = nt(q, k_all[:seen]) * SCALE
            pieces = [s[:, :BLOCK] + off]
            if half:
                pieces.append(s[:, BLOCK : BLOCK + ROWS])
            pieces.append(jnp.where(tri, s[:, seen - ROWS :], FAR))
            s = jnp.concatenate(pieces, axis=1)
            m = jnp.max(s, axis=1, keepdims=True)
            p = jnp.exp(s - m).astype(BF16)
            r = nn(p, v_all[:seen])
            co_v[r0 : r0 + ROWS, j * HEAD : (j + 1) * HEAD] = (r[:, :HEAD] / r[:, HEAD:]).astype(BF16)
        if j % 2:
            cols = slice((j - 1) * HEAD, (j + 1) * HEAD)
            pltpu.make_async_copy(co_v.at[:, cols], ctx_out.at[:, cols], out_sem).start()

    arrived(co_v, out_sem)
    arrived(sxs.at[six], sx_sem.at[PIECES])
    arrived(pxs, sp_sem.at[PIECES])
    arrived(hs.at[others], hs_sem)
    for i in range(PIECES):
        arrived(sx.at[i, six], sx_sem.at[i])
        arrived(px.at[i], sp_sem.at[i])
        arrived(att.at[i, others], gxs_sem.at[i])

    @pl.when(~owns_odd)
    def _():
        arrived(szs, sz_sem.at[PIECES])
        for i in range(PIECES):
            arrived(sz.at[i], sz_sem.at[i])

    for i in range(PIECES):

        @pl.when(owns_even)
        def _():
            arrived(att.at[i], gzs_sem.at[i])

        @pl.when(owns_odd)
        def _():
            arrived(att.at[i, others], gzs_sem.at[i])

    @pl.when(c == 0)
    def _():
        anchor_sent(0, 3)

    @pl.when(at_foot)
    def _():
        anchor_sent(1, 7)

    @pl.when(core == 0)
    def _():
        @pl.when((z == 0) & (x > 0))
        def _():
            anchor_sent(2, 2)

        @pl.when((z > 0) | (x == 0))
        def _():
            anchor_sent(2, 3)

        anchor_sent(3, 4)

    arrived(hr.at[others], hr_sem)
    result = hs[h].astype(F32)
    for slot in range(1, 8):
        result = result + hr[slot].astype(F32)
    opt_out[...] = result.astype(BF16)


def put_out(co, oo, ctx_out, opt_out, sem):
    copies = [pltpu.make_async_copy(oo, opt_out, sem.at[8])]
    for n in range(8):
        rows = pl.ds(n * 32, 32)
        copies.append(pltpu.make_async_copy(co.at[rows], ctx_out.at[rows], sem.at[n]))
    for copy in copies:
        copy.start()
    for copy in copies:
        copy.wait()


def layer(cq, ck, cv, oq, ok, ov, seg, w):
    vmem, dma = pltpu.VMEM, pltpu.SemaphoreType.DMA
    anywhere = pl.BlockSpec(memory_space=pl.ANY)
    parts = pl.pallas_call(
        kernel,
        name="star_attention",
        out_shape=(vmem((BLOCK, GROUPS * HEAD), BF16), vmem((ROWS // 8, HEAD), BF16)),
        in_specs=[anywhere] * 8,
        out_specs=(anywhere, pl.BlockSpec(memory_space=vmem)),
        scratch_shapes=[
            vmem((BLOCK, GROUPS * HEAD), BF16),
            vmem((2, 2 * BLOCK, HEAD), BF16),
            vmem((BLOCK, GROUPS * HEAD), BF16),
            vmem((ROWS, GROUPS * HEAD), BF16),
            vmem((ROWS, HEAD), BF16),
            vmem((ROWS, HEAD), BF16),
            vmem((1, ROWS), jnp.int32),
            vmem((GROUPS * HEAD, HEAD), BF16),
            vmem((PIECES, HEAD, GROUPS * PIECE), BF16),
            vmem((PIECES, 8, PIECE, ROWS), BF16),
            vmem((8, 2, ROWS), F32),
            vmem((PIECES, PIECE, ROWS), BF16),
            vmem((2, ROWS), F32),
            vmem((PIECES, 8, PIECE, ROWS), BF16),
            vmem((8, 2, ROWS), F32),
            vmem((PIECES, PIECE, ROWS), BF16),
            vmem((2, ROWS), F32),
            vmem((PIECES, 8, PIECE, ROWS), BF16),
            vmem((8, 2, ROWS), F32),
            vmem((PIECES, PIECE, ROWS), BF16),
            vmem((PIECES, 8, PIECE, ROWS), BF16),
            vmem((8, 16, HEAD), BF16),
            vmem((8, 16, HEAD), BF16),
            dma((7,)),
            dma(()),
            dma((PIECES + 1,)),
            dma((PIECES + 1,)),
            dma((PIECES + 1,)),
            dma((PIECES + 1,)),
            dma((PIECES + 1,)),
            dma((PIECES + 1,)),
            dma((PIECES,)),
            dma((PIECES,)),
            dma((PIECES,)),
            dma((PIECES,)),
            dma(()),
            dma(()),
            dma((4,)),
            dma((4,)),
            pltpu.SemaphoreType.REGULAR((4,)),
            pltpu.SemaphoreType.REGULAR,
        ],
        compiler_params=pltpu.CompilerParams(collective_id=0, has_side_effects=True),
    )(cq, ck, cv, oq, ok, ov, seg.reshape(1, ROWS), w)
    return pl.pallas_call(
        put_out,
        name="put_out",
        out_shape=(
            jax.ShapeDtypeStruct((BLOCK, GROUPS * HEAD), BF16),
            jax.ShapeDtypeStruct((ROWS // 8, HEAD), BF16),
        ),
        in_specs=[pl.BlockSpec(memory_space=vmem)] * 2,
        out_specs=(anywhere, anywhere),
        scratch_shapes=[dma((9,))],
    )(*[pltpu.with_memory_space_constraint(part, vmem) for part in parts])


def solution(mesh):
    placed = (
        P("ctx", "head"),
        P("ctx", "head"),
        P("ctx", "head"),
        P(None, "head"),
        P(None, "head"),
        P(None, "head"),
        P(),
        P("head", "ctx"),
    )
    return jax.shard_map(
        layer,
        mesh=mesh,
        in_specs=placed,
        out_specs=(P("ctx", "head"), P("head", "ctx")),
        check_vma=False,
    )
```

```python
import functools

import jax
import jax.numpy as jnp
from jax import lax
from jax.experimental import pallas as pl
from jax.experimental.pallas import tpu as pltpu
from jax.sharding import PartitionSpec as P

MESH = pl.DeviceIdType.MESH
HEAD = 128
ROWS = 128
BLOCK = 256
GROUPS = 8
NZ = 8
OWNER_Z = 3
PIECES = 4
PIECE = HEAD // PIECES
QUARTER = BLOCK // 4
SCALE = HEAD ** (-0.5)
FAR = -1e30
F32 = jnp.float32
BF16 = jnp.bfloat16


def nt(a, b):
    return lax.dot_general(a, b, (((1,), (1,)), ((), ())), preferred_element_type=F32)


def nn(a, b):
    return lax.dot_general(a, b, (((1,), (0,)), ((), ())), preferred_element_type=F32)


def kernel(
    cq, ck, cv, oq, ok, ov, seg, w,
    ctx_out, opt_out,
    cq_v, kv, co_v, oq_v, ok_v, ov_v, seg_v, w_v, wt,
    sx, sxs, px, pxs, rx, rxs, sz, szs, rz, rzs, owned, att, hs, hr,
    in_sem, out_sem, sp_sem, rp_sem, sx_sem, rx_sem, sz_sem, rz_sem,
    gzs_sem, gzr_sem, gxs_sem, gxr_sem, hs_sem, hr_sem, as_sem, ar_sem, near_sem, pair_sem,
):
    c = lax.axis_index("ctx")
    h = lax.axis_index("head")
    z, g = c // 8, c % 8
    x, core = g // 2, g % 2
    zh, y = h // 4, h % 4
    zo = OWNER_Z + core
    owner = zo * 8 + x * 2 + 1
    partner = z * 8 + x * 2 + (core + 1) % 2
    owns_even = (core == 1) & (z == OWNER_Z)
    owns_odd = (core == 1) & (z == OWNER_Z + 1)
    owned_head = x * 2 + (z + OWNER_Z) % 2

    def at_ctx(cc):
        return {"ctx": cc, "head": h}

    def x_peer(dx, dc):
        return z * 8 + ((x + dx) % 4) * 2 + (core + dc) % 2

    def head_peer(kz, ky):
        return ((zh + kz) % 2) * 4 + (y + ky) % 4

    def along_z(k):
        zz = (zh * NZ + z + k) % (2 * NZ)
        return {"ctx": (zz % NZ) * 8 + g, "head": (zz // NZ) * 4 + y}

    def tell(sem, target):
        pl.semaphore_signal(sem, inc=1, device_id=target, device_id_type=MESH)

    own = pl.ds(BLOCK, BLOCK)
    anchor = pl.ds(0, BLOCK)
    def arrived(ref, sem):
        pltpu.make_async_copy(ref, ref, sem).wait()

    def query_load(dx):
        cols = pl.ds(pl.multiple_of(((x + dx) % 4) * 2 * HEAD, 2 * HEAD), 2 * HEAD)
        return pltpu.make_async_copy(oq.at[:, cols], oq_v.at[:, cols], in_sem.at[0 if dx == 2 else 1])

    pltpu.make_async_copy(ck, kv.at[0, own], in_sem.at[0]).start()
    query_load(2).start()
    pltpu.make_async_copy(cv, kv.at[1, own], in_sem.at[0]).start()
    barrier = pltpu.get_barrier_semaphore()
    for slot in range(1, 8):
        tell(barrier, at_ctx(x_peer(slot // 2, slot % 2)))
    for k in (1, 15):
        tell(barrier, along_z(k))
    for k in range(1, 4):
        tell(barrier, {"ctx": c, "head": head_peer(0, k)})
    for dx in (1, 3, 0):
        query_load(dx).start()
    pltpu.make_async_copy(ok, ok_v, in_sem.at[2]).start()
    pltpu.make_async_copy(ov, ov_v, in_sem.at[2]).start()
    pltpu.make_async_copy(seg, seg_v, in_sem.at[3]).start()
    pltpu.make_async_copy(w, w_v, in_sem.at[4]).start()
    pltpu.make_async_copy(cq, cq_v, in_sem.at[5]).start()

    @pl.when(c == 0)
    def _():
        pltpu.make_async_copy(ck, kv.at[0, anchor], in_sem.at[6]).start()
        pltpu.make_async_copy(cv, kv.at[1, anchor], in_sem.at[6]).start()

    def anchor_copy(q, n, target):
        ref = kv.at[:, pl.ds(pl.multiple_of(q * QUARTER, QUARTER), QUARTER)]
        return pltpu.make_async_remote_copy(
            src_ref=ref, dst_ref=ref, send_sem=as_sem.at[n], recv_sem=ar_sem.at[q],
            device_id=at_ctx(target), device_id_type=MESH,
        )

    def anchor_sent(n, quarters):
        arrived(kv.at[:, 0 : quarters * QUARTER], as_sem.at[n])

    arrived(oq_v.at[:, 0 : 6 * HEAD], in_sem.at[0])
    k_own = kv[0, own, :]
    vt_own = kv[1, own, :].astype(F32).T.astype(BF16)

    def partial(q, keys, vt, mask=None):
        s = nt(keys, q) * SCALE
        if mask is not None:
            s = jnp.where(mask, s, FAR)
        m = jnp.max(s, axis=0, keepdims=True)
        p = jnp.exp(s - m)
        if mask is not None:
            p = jnp.where(mask, p, 0.0)
        return m, jnp.sum(p, axis=0, keepdims=True), nn(vt, p.astype(BF16))

    def x_copy(i, slot, target):
        src, dst = (sxs, rxs) if i == PIECES else (sx.at[i], rx.at[i])
        return pltpu.make_async_remote_copy(
            src_ref=src.at[slot], dst_ref=dst.at[slot],
            send_sem=sx_sem.at[i], recv_sem=rx_sem.at[i],
            device_id=at_ctx(target), device_id_type=MESH,
        )

    others = pl.ds(1, 7)
    six = pl.ds(1, 6)
    senders = (1, 2, 3, 4, 6, 7)

    def piece(i):
        return slice(i * PIECE, (i + 1) * PIECE)

    def option_heads(slots):
        qs = []
        for slot in slots:
            gd = ((x + slot // 2) % 4) * 2 + (core + slot % 2) % 2
            qs.append(oq_v[:, pl.ds(pl.multiple_of(gd * HEAD, HEAD), HEAD)])
        m, l, mix = partial(jnp.concatenate(qs, axis=0), k_own, vt_own)
        for n, slot in enumerate(slots):
            lanes = slice(n * ROWS, (n + 1) * ROWS)
            for i in range(PIECES):
                sx[i, slot] = mix[piece(i), lanes].astype(BF16)
            sxs[slot, 0:1, :] = m[:, lanes]
            sxs[slot, 1:2, :] = l[:, lanes]

    def send_heads(i, slots):
        for slot in slots:
            x_copy(i, slot, x_peer(slot // 2, slot % 2)).start()

    def pair_copy(i):
        src, dst = (sxs, pxs) if i == PIECES else (sx.at[i], px.at[i])
        return pltpu.make_async_remote_copy(
            src_ref=src.at[5], dst_ref=dst, send_sem=sp_sem.at[i], recv_sem=rp_sem.at[i],
            device_id=at_ctx(partner), device_id_type=MESH,
        )

    option_heads((5, 4))
    pl.semaphore_wait(barrier, 12)
    for i in (PIECES, *range(PIECES)):
        pair_copy(i).start()
    for k in (1, 15):
        tell(near_sem.at[0], along_z(k))

    arrived(oq_v.at[:, 0 : 6 * HEAD], in_sem.at[1])
    option_heads((2, 3, 6, 7))
    send_heads(PIECES, (2, 3, 6, 7))
    send_heads(0, (2, 3, 6, 7))

    arrived(pxs, rp_sem.at[PIECES])
    m_here, m_there = sxs[4, 0:1, :], pxs[0:1, :]
    m_pair = jnp.maximum(m_here, m_there)
    f_here, f_there = jnp.exp(m_here - m_pair), jnp.exp(m_there - m_pair)
    l_pair = f_here * sxs[4, 1:2, :] + f_there * pxs[1:2, :]
    sxs[4, 0:1, :] = m_pair
    sxs[4, 1:2, :] = l_pair
    for i in range(PIECES):
        arrived(px.at[i], rp_sem.at[i])
        sx[i, 4] = (f_here * sx[i, 4].astype(F32) + f_there * px[i].astype(F32)).astype(BF16)
    send_heads(PIECES, (4,))
    for i in range(PIECES):
        send_heads(i, (4,))
    option_heads((1, 0))
    send_heads(PIECES, (1,))
    send_heads(0, (1,))
    for i in range(1, PIECES):
        send_heads(i, (2, 3, 6, 7, 1))

    @pl.when(c == 0)
    def _():
        arrived(kv.at[:, anchor], in_sem.at[6])
        for q in (2, 1, 3):
            anchor_copy(q, 0, q * 2).start()

    pl.semaphore_wait(near_sem.at[0], 2)
    for k in (2, 14):
        tell(near_sem.at[1], along_z(k))

    arrived(kv.at[0, own], in_sem.at[2])
    arrived(seg_v, in_sem.at[3])
    seg_row = jnp.broadcast_to(seg_v[...].astype(F32), (ROWS, ROWS))
    seg_col = seg_row.T
    key_at = lax.broadcasted_iota(jnp.int32, (ROWS, ROWS), 0)
    row_at = lax.broadcasted_iota(jnp.int32, (ROWS, ROWS), 1)
    visible = (seg_row == seg_col) & (row_at >= key_at)
    q_own = oq_v[:, pl.ds(pl.multiple_of(owned_head * HEAD, HEAD), HEAD)]
    vt_self = ov_v[...].astype(F32).T.astype(BF16)
    self_part = partial(q_own, ok_v[...], vt_self, visible)

    arrived(w_v, in_sem.at[4])
    for i in range(PIECES):
        rows = [w_v[j * HEAD + i * PIECE : j * HEAD + (i + 1) * PIECE, :] for j in range(GROUPS)]
        wt[i] = jnp.concatenate(rows, axis=0).astype(F32).T.astype(BF16)

    pl.semaphore_wait(near_sem.at[1], 2)
    for k in (4, 12):
        tell(near_sem.at[2], along_z(k))

    @pl.when(core == 1)
    def _():
        tell(pair_sem, at_ctx(partner))

    def factors_of(tops):
        top = functools.reduce(jnp.maximum, tops)
        return top, [jnp.exp(m - top) for m in tops]

    def z_copy(i, k, target):
        src, dst = (szs, rzs) if i == PIECES else (sz.at[i], rz.at[i])
        return pltpu.make_async_remote_copy(
            src_ref=src, dst_ref=dst.at[k], send_sem=sz_sem.at[i], recv_sem=rz_sem.at[i],
            device_id=at_ctx(target), device_id_type=MESH,
        )

    arrived(rxs.at[six], rx_sem.at[PIECES])
    top, factors = factors_of([sxs[0, 0:1, :]] + [rxs[k, 0:1, :] for k in senders])
    total = factors[0] * sxs[0, 1:2, :]
    for n, k in enumerate(senders):
        total = total + factors[n + 1] * rxs[k, 1:2, :]

    @pl.when(core == 0)
    def _():
        pl.semaphore_wait(pair_sem, 1)

    @pl.when(~owns_odd)
    def _():
        szs[0:1, :] = top
        szs[1:2, :] = total
        z_copy(PIECES, z, owner).start()

    @pl.when(owns_odd)
    def _():
        rzs[OWNER_Z + 1, 0:1, :] = top
        rzs[OWNER_Z + 1, 1:2, :] = total

    for i in range(PIECES):
        arrived(rx.at[i, six], rx_sem.at[i])
        mix = factors[0] * sx[i, 0].astype(F32)
        for n, k in enumerate(senders):
            mix = mix + factors[n + 1] * rx[i, k].astype(F32)

        @pl.when(~owns_odd)
        def _():
            sz[i] = mix.astype(BF16)
            z_copy(i, z, owner).start()

        @pl.when(owns_odd)
        def _():
            rz[i, OWNER_Z + 1] = mix.astype(BF16)

    at_foot = (z == 0) & (core == 0)

    def anchor_up():
        @pl.when(x > 0)
        def _():
            anchor_copy(x, 0, c).wait_recv()

        for k in (7, 6, 5, 4, 3, 2, 1):
            anchor_copy(x, 1, k * 8 + g).start()

    pl.semaphore_wait(near_sem.at[2], 2)
    for k in (1, 15):
        tell(near_sem.at[3], along_z(k))

    @pl.when(at_foot)
    def _():
        anchor_up()

    def gz_copy(i, target):
        return pltpu.make_async_remote_copy(
            src_ref=owned.at[i], dst_ref=att.at[i, owned_head], send_sem=gzs_sem.at[i], recv_sem=gzr_sem.at[i],
            device_id=at_ctx(target), device_id_type=MESH,
        )

    def gx_copy(i, target):
        return pltpu.make_async_remote_copy(
            src_ref=att.at[i, g], dst_ref=att.at[i, g], send_sem=gxs_sem.at[i], recv_sem=gxr_sem.at[i],
            device_id=at_ctx(target), device_id_type=MESH,
        )

    def gx_send(i):
        for slot in (4, 5, 2, 3, 6, 7, 1):
            gx_copy(i, x_peer(slot // 2, slot % 2)).start()

    def column_arrived(ref, sem):
        @pl.when(owns_even)
        def _():
            arrived(ref, sem)

        @pl.when(owns_odd)
        def _():
            arrived(ref.at[others], sem)

    @pl.when(owns_even | owns_odd)
    def _():
        self_top, self_total, self_mix = self_part
        column_arrived(rzs, rz_sem.at[PIECES])
        _, parts = factors_of([self_top] + [rzs[k, 0:1, :] for k in range(NZ)])
        whole = parts[0] * self_total
        for k in range(NZ):
            whole = whole + parts[k + 1] * rzs[k, 1:2, :]
        for i in range(PIECES):
            column_arrived(rz.at[i], rz_sem.at[i])
            summed = parts[0] * self_mix[piece(i)]
            for k in range(NZ):
                summed = summed + parts[k + 1] * rz[i, k].astype(F32)
            owned[i] = (summed / whole).astype(BF16)

            @pl.when(owns_odd)
            def _():
                att[i, g] = owned[i]

            for k in (0, 1, 2, 7, 3, 6, 5):
                gz_copy(i, k * 8 + owned_head).start()

            @pl.when(owns_even)
            def _():
                gz_copy(i, 4 * 8 + owned_head).start()

    @pl.when(owns_odd)
    def _():
        for i in range(PIECES):
            gx_send(i)

    @pl.when(~owns_odd)
    def _():
        for i in range(PIECES):
            arrived(att.at[i, 0], gzr_sem.at[i])
            gx_send(i)

    pl.semaphore_wait(near_sem.at[3], 2)
    arrived(cq_v, in_sem.at[5])

    projected = None
    for i in range(PIECES):
        arrived(att.at[i, others], gxr_sem.at[i])
        share = nn(wt[i], att[i].reshape(GROUPS * PIECE, ROWS))
        projected = share if projected is None else projected + share
    hs[...] = projected.T.astype(BF16).reshape(8, 16, HEAD)

    def h_copy(slot, source, target):
        return pltpu.make_async_remote_copy(
            src_ref=hs.at[source], dst_ref=hr.at[slot], send_sem=hs_sem, recv_sem=hr_sem,
            device_id={"ctx": c, "head": target}, device_id_type=MESH,
        )

    for slot in (6, 5, 7, 4, 2, 1, 3):
        peer = head_peer(slot // 4, slot % 4)
        h_copy(slot, peer, peer).start()

    @pl.when(core == 0)
    def _():
        @pl.when(z > 0)
        def _():
            anchor_copy(x, 0, c).wait_recv()

        for k in (2, 1, 3):

            @pl.when((z > 0) | ((x + k) % 4 > 0))
            def _():
                anchor_copy(x, 2, z * 8 + ((x + k) % 4) * 2).start()

        anchor_copy(x, 3, c + 1).start()

    @pl.when((core == 0) & (c > 0))
    def _():
        for k in (1, 3, 2):
            q = (x + k) % 4
            anchor_copy(q, 0, c).wait_recv()
            anchor_copy(q, 3, c + 1).start()

    @pl.when(c == 0)
    def _():
        for q in range(1, 4):
            anchor_copy(q, 3, 1).start()

    @pl.when(core == 1)
    def _():
        for q in range(4):
            anchor_copy(q, 0, c).wait_recv()

    off = jnp.where(c > 0, 0.0, FAR).astype(F32)
    k_all = kv[0]
    v_all = jnp.concatenate([kv[1], jnp.ones((2 * BLOCK, HEAD), BF16)], axis=1)
    tri = lax.broadcasted_iota(jnp.int32, (ROWS, ROWS), 0) >= lax.broadcasted_iota(jnp.int32, (ROWS, ROWS), 1)
    for j in range(GROUPS):
        for half in range(2):
            r0 = half * ROWS
            seen = BLOCK + r0 + ROWS
            q = cq_v[r0 : r0 + ROWS, j * HEAD : (j + 1) * HEAD]
            s = nt(q, k_all[:seen]) * SCALE
            pieces = [s[:, :BLOCK] + off]
            if half:
                pieces.append(s[:, BLOCK : BLOCK + ROWS])
            pieces.append(jnp.where(tri, s[:, seen - ROWS :], FAR))
            s = jnp.concatenate(pieces, axis=1)
            m = jnp.max(s, axis=1, keepdims=True)
            p = jnp.exp(s - m).astype(BF16)
            r = nn(p, v_all[:seen])
            co_v[r0 : r0 + ROWS, j * HEAD : (j + 1) * HEAD] = (r[:, :HEAD] / r[:, HEAD:]).astype(BF16)
        if j % 2:
            cols = slice((j - 1) * HEAD, (j + 1) * HEAD)
            pltpu.make_async_copy(co_v.at[:, cols], ctx_out.at[:, cols], out_sem).start()

    arrived(co_v, out_sem)
    arrived(sxs.at[six], sx_sem.at[PIECES])
    arrived(pxs, sp_sem.at[PIECES])
    arrived(hs.at[others], hs_sem)
    for i in range(PIECES):
        arrived(sx.at[i, six], sx_sem.at[i])
        arrived(px.at[i], sp_sem.at[i])
        arrived(att.at[i, others], gxs_sem.at[i])

    @pl.when(~owns_odd)
    def _():
        arrived(szs, sz_sem.at[PIECES])
        for i in range(PIECES):
            arrived(sz.at[i], sz_sem.at[i])

    for i in range(PIECES):

        @pl.when(owns_even)
        def _():
            arrived(att.at[i], gzs_sem.at[i])

        @pl.when(owns_odd)
        def _():
            arrived(att.at[i, others], gzs_sem.at[i])

    @pl.when(c == 0)
    def _():
        anchor_sent(0, 3)

    @pl.when(at_foot)
    def _():
        anchor_sent(1, 7)

    @pl.when(core == 0)
    def _():
        @pl.when((z == 0) & (x > 0))
        def _():
            anchor_sent(2, 2)

        @pl.when((z > 0) | (x == 0))
        def _():
            anchor_sent(2, 3)

        anchor_sent(3, 4)

    arrived(hr.at[others], hr_sem)
    result = hs[h].astype(F32)
    for slot in range(1, 8):
        result = result + hr[slot].astype(F32)
    opt_out[...] = result.astype(BF16)


def put_out(co, oo, ctx_out, opt_out, sem):
    copies = [pltpu.make_async_copy(oo, opt_out, sem.at[0]), pltpu.make_async_copy(co, ctx_out, sem.at[1])]
    for copy in copies:
        copy.start()
    for copy in copies:
        copy.wait()


def layer(cq, ck, cv, oq, ok, ov, seg, w):
    vmem, dma = pltpu.VMEM, pltpu.SemaphoreType.DMA
    anywhere = pl.BlockSpec(memory_space=pl.ANY)
    parts = pl.pallas_call(
        kernel,
        name="star_attention",
        out_shape=(vmem((BLOCK, GROUPS * HEAD), BF16), vmem((ROWS // 8, HEAD), BF16)),
        in_specs=[anywhere] * 8,
        out_specs=(anywhere, pl.BlockSpec(memory_space=vmem)),
        scratch_shapes=[
            vmem((BLOCK, GROUPS * HEAD), BF16),
            vmem((2, 2 * BLOCK, HEAD), BF16),
            vmem((BLOCK, GROUPS * HEAD), BF16),
            vmem((ROWS, GROUPS * HEAD), BF16),
            vmem((ROWS, HEAD), BF16),
            vmem((ROWS, HEAD), BF16),
            vmem((1, ROWS), jnp.int32),
            vmem((GROUPS * HEAD, HEAD), BF16),
            vmem((PIECES, HEAD, GROUPS * PIECE), BF16),
            vmem((PIECES, 8, PIECE, ROWS), BF16),
            vmem((8, 2, ROWS), F32),
            vmem((PIECES, PIECE, ROWS), BF16),
            vmem((2, ROWS), F32),
            vmem((PIECES, 8, PIECE, ROWS), BF16),
            vmem((8, 2, ROWS), F32),
            vmem((PIECES, PIECE, ROWS), BF16),
            vmem((2, ROWS), F32),
            vmem((PIECES, 8, PIECE, ROWS), BF16),
            vmem((8, 2, ROWS), F32),
            vmem((PIECES, PIECE, ROWS), BF16),
            vmem((PIECES, 8, PIECE, ROWS), BF16),
            vmem((8, 16, HEAD), BF16),
            vmem((8, 16, HEAD), BF16),
            dma((7,)),
            dma(()),
            dma((PIECES + 1,)),
            dma((PIECES + 1,)),
            dma((PIECES + 1,)),
            dma((PIECES + 1,)),
            dma((PIECES + 1,)),
            dma((PIECES + 1,)),
            dma((PIECES,)),
            dma((PIECES,)),
            dma((PIECES,)),
            dma((PIECES,)),
            dma(()),
            dma(()),
            dma((4,)),
            dma((4,)),
            pltpu.SemaphoreType.REGULAR((4,)),
            pltpu.SemaphoreType.REGULAR,
        ],
        compiler_params=pltpu.CompilerParams(collective_id=0, has_side_effects=True),
    )(cq, ck, cv, oq, ok, ov, seg.reshape(1, ROWS), w)
    return pl.pallas_call(
        put_out,
        name="put_out",
        out_shape=(
            jax.ShapeDtypeStruct((BLOCK, GROUPS * HEAD), BF16),
            jax.ShapeDtypeStruct((ROWS // 8, HEAD), BF16),
        ),
        in_specs=[pl.BlockSpec(memory_space=vmem)] * 2,
        out_specs=(anywhere, anywhere),
        scratch_shapes=[dma((2,))],
    )(*[pltpu.with_memory_space_constraint(part, vmem) for part in parts])


def solution(mesh):
    placed = (
        P("ctx", "head"),
        P("ctx", "head"),
        P("ctx", "head"),
        P(None, "head"),
        P(None, "head"),
        P(None, "head"),
        P(),
        P("head", "ctx"),
    )
    return jax.shard_map(
        layer,
        mesh=mesh,
        in_specs=placed,
        out_specs=(P("ctx", "head"), P("head", "ctx")),
        check_vma=False,
    )
```

```python
import functools

import jax
import jax.numpy as jnp
from jax import lax
from jax.experimental import pallas as pl
from jax.experimental.pallas import tpu as pltpu
from jax.sharding import PartitionSpec as P

MESH = pl.DeviceIdType.MESH
HEAD = 128
ROWS = 128
BLOCK = 256
GROUPS = 8
NZ = 8
OWNER_Z = 3
PIECES = 4
PIECE = HEAD // PIECES
QUARTER = BLOCK // 4
SCALE = HEAD ** (-0.5)
FAR = -1e30
F32 = jnp.float32
BF16 = jnp.bfloat16


def nt(a, b):
    return lax.dot_general(a, b, (((1,), (1,)), ((), ())), preferred_element_type=F32)


def nn(a, b):
    return lax.dot_general(a, b, (((1,), (0,)), ((), ())), preferred_element_type=F32)


def kernel(
    cq, ck, cv, oq, ok, ov, seg, w,
    ctx_out, opt_out,
    cq_v, kv, co_v, oq_v, ok_v, ov_v, seg_v, w_v, wt,
    sx, sxs, px, pxs, rx, rxs, sz, szs, rz, rzs, owned, att, hs, hr,
    in_sem, out_sem, sp_sem, rp_sem, sx_sem, rx_sem, sz_sem, rz_sem,
    gzs_sem, gzr_sem, gxs_sem, gxr_sem, hs_sem, hr_sem, as_sem, ar_sem, near_sem, pair_sem,
):
    c = lax.axis_index("ctx")
    h = lax.axis_index("head")
    z, g = c // 8, c % 8
    x, core = g // 2, g % 2
    zh, y = h // 4, h % 4
    zo = OWNER_Z + core
    owner = zo * 8 + x * 2 + 1
    partner = z * 8 + x * 2 + (core + 1) % 2
    owns_even = (core == 1) & (z == OWNER_Z)
    owns_odd = (core == 1) & (z == OWNER_Z + 1)
    owned_head = x * 2 + (z + OWNER_Z) % 2

    def at_ctx(cc):
        return {"ctx": cc, "head": h}

    def x_peer(dx, dc):
        return z * 8 + ((x + dx) % 4) * 2 + (core + dc) % 2

    def head_peer(kz, ky):
        return ((zh + kz) % 2) * 4 + (y + ky) % 4

    def along_z(k):
        zz = (zh * NZ + z + k) % (2 * NZ)
        return {"ctx": (zz % NZ) * 8 + g, "head": (zz // NZ) * 4 + y}

    def tell(sem, target):
        pl.semaphore_signal(sem, inc=1, device_id=target, device_id_type=MESH)

    own = pl.ds(BLOCK, BLOCK)
    anchor = pl.ds(0, BLOCK)
    def arrived(ref, sem):
        pltpu.make_async_copy(ref, ref, sem).wait()

    def query_load(dx):
        cols = pl.ds(pl.multiple_of(((x + dx) % 4) * 2 * HEAD, 2 * HEAD), 2 * HEAD)
        return pltpu.make_async_copy(oq.at[:, cols], oq_v.at[:, cols], in_sem.at[0 if dx == 2 else 1])

    pltpu.make_async_copy(ck, kv.at[0, own], in_sem.at[0]).start()
    query_load(2).start()
    pltpu.make_async_copy(cv, kv.at[1, own], in_sem.at[0]).start()
    barrier = pltpu.get_barrier_semaphore()
    for slot in range(1, 8):
        tell(barrier, at_ctx(x_peer(slot // 2, slot % 2)))
    for k in (1, 15):
        tell(barrier, along_z(k))
    for k in range(1, 4):
        tell(barrier, {"ctx": c, "head": head_peer(0, k)})
    for dx in (1, 3, 0):
        query_load(dx).start()
    pltpu.make_async_copy(ok, ok_v, in_sem.at[2]).start()
    pltpu.make_async_copy(ov, ov_v, in_sem.at[2]).start()
    pltpu.make_async_copy(seg, seg_v, in_sem.at[3]).start()
    pltpu.make_async_copy(w, w_v, in_sem.at[4]).start()
    pltpu.make_async_copy(cq, cq_v, in_sem.at[5]).start()

    @pl.when(c == 0)
    def _():
        pltpu.make_async_copy(ck, kv.at[0, anchor], in_sem.at[6]).start()
        pltpu.make_async_copy(cv, kv.at[1, anchor], in_sem.at[6]).start()

    def anchor_copy(q, n, target):
        ref = kv.at[:, pl.ds(pl.multiple_of(q * QUARTER, QUARTER), QUARTER)]
        return pltpu.make_async_remote_copy(
            src_ref=ref, dst_ref=ref, send_sem=as_sem.at[n], recv_sem=ar_sem.at[q],
            device_id=at_ctx(target), device_id_type=MESH,
        )

    def anchor_sent(n, quarters):
        arrived(kv.at[:, 0 : quarters * QUARTER], as_sem.at[n])

    arrived(oq_v.at[:, 0 : 6 * HEAD], in_sem.at[0])
    k_own = kv[0, own, :]
    vt_own = kv[1, own, :].astype(F32).T.astype(BF16)

    def partial(q, keys, vt, mask=None):
        s = nt(keys, q) * SCALE
        if mask is not None:
            s = jnp.where(mask, s, FAR)
        m = jnp.max(s, axis=0, keepdims=True)
        p = jnp.exp(s - m)
        if mask is not None:
            p = jnp.where(mask, p, 0.0)
        return m, jnp.sum(p, axis=0, keepdims=True), nn(vt, p.astype(BF16))

    def x_copy(i, slot, target):
        src, dst = (sxs, rxs) if i == PIECES else (sx.at[i], rx.at[i])
        return pltpu.make_async_remote_copy(
            src_ref=src.at[slot], dst_ref=dst.at[slot],
            send_sem=sx_sem.at[i // PIECES], recv_sem=rx_sem.at[i],
            device_id=at_ctx(target), device_id_type=MESH,
        )

    others = pl.ds(1, 7)
    six = pl.ds(1, 6)
    senders = (1, 2, 3, 4, 6, 7)

    def piece(i):
        return slice(i * PIECE, (i + 1) * PIECE)

    def option_heads(slots):
        qs = []
        for slot in slots:
            gd = ((x + slot // 2) % 4) * 2 + (core + slot % 2) % 2
            qs.append(oq_v[:, pl.ds(pl.multiple_of(gd * HEAD, HEAD), HEAD)])
        m, l, mix = partial(jnp.concatenate(qs, axis=0), k_own, vt_own)
        for n, slot in enumerate(slots):
            lanes = slice(n * ROWS, (n + 1) * ROWS)
            for i in range(PIECES):
                sx[i, slot] = mix[piece(i), lanes].astype(BF16)
            sxs[slot, 0:1, :] = m[:, lanes]
            sxs[slot, 1:2, :] = l[:, lanes]

    def send_heads(i, slots):
        for slot in slots:
            x_copy(i, slot, x_peer(slot // 2, slot % 2)).start()

    def pair_copy(i):
        src, dst = (sxs, pxs) if i == PIECES else (sx.at[i], px.at[i])
        return pltpu.make_async_remote_copy(
            src_ref=src.at[5], dst_ref=dst, send_sem=sp_sem.at[i // PIECES], recv_sem=rp_sem.at[i // PIECES],
            device_id=at_ctx(partner), device_id_type=MESH,
        )

    option_heads((5, 4))
    pl.semaphore_wait(barrier, 12)
    for i in (PIECES, *range(PIECES)):
        pair_copy(i).start()
    for k in (1, 15):
        tell(near_sem.at[0], along_z(k))

    arrived(oq_v.at[:, 0 : 6 * HEAD], in_sem.at[1])
    option_heads((2, 3, 6, 7))
    send_heads(PIECES, (2, 3, 6, 7))
    send_heads(0, (2, 3, 6, 7))

    arrived(pxs, rp_sem.at[1])
    m_here, m_there = sxs[4, 0:1, :], pxs[0:1, :]
    m_pair = jnp.maximum(m_here, m_there)
    f_here, f_there = jnp.exp(m_here - m_pair), jnp.exp(m_there - m_pair)
    l_pair = f_here * sxs[4, 1:2, :] + f_there * pxs[1:2, :]
    sxs[4, 0:1, :] = m_pair
    sxs[4, 1:2, :] = l_pair
    arrived(px, rp_sem.at[0])
    for i in range(PIECES):
        sx[i, 4] = (f_here * sx[i, 4].astype(F32) + f_there * px[i].astype(F32)).astype(BF16)
    send_heads(PIECES, (4,))
    send_heads(0, (4,))
    option_heads((1, 0))
    send_heads(PIECES, (1,))
    send_heads(0, (1,))
    for i in range(1, PIECES):
        send_heads(i, (4, 2, 3, 6, 7, 1))

    @pl.when(c == 0)
    def _():
        arrived(kv.at[:, anchor], in_sem.at[6])
        for q in (2, 1, 3):
            anchor_copy(q, 0, q * 2).start()

    pl.semaphore_wait(near_sem.at[0], 2)
    for k in (2, 14):
        tell(near_sem.at[1], along_z(k))

    arrived(kv.at[0, own], in_sem.at[2])
    arrived(seg_v, in_sem.at[3])
    seg_row = jnp.broadcast_to(seg_v[...].astype(F32), (ROWS, ROWS))
    seg_col = seg_row.T
    key_at = lax.broadcasted_iota(jnp.int32, (ROWS, ROWS), 0)
    row_at = lax.broadcasted_iota(jnp.int32, (ROWS, ROWS), 1)
    visible = (seg_row == seg_col) & (row_at >= key_at)
    q_own = oq_v[:, pl.ds(pl.multiple_of(owned_head * HEAD, HEAD), HEAD)]
    vt_self = ov_v[...].astype(F32).T.astype(BF16)
    self_part = partial(q_own, ok_v[...], vt_self, visible)

    arrived(w_v, in_sem.at[4])
    for i in range(PIECES):
        rows = [w_v[j * HEAD + i * PIECE : j * HEAD + (i + 1) * PIECE, :] for j in range(GROUPS)]
        wt[i] = jnp.concatenate(rows, axis=0).astype(F32).T.astype(BF16)

    pl.semaphore_wait(near_sem.at[1], 2)
    for k in (4, 12):
        tell(near_sem.at[2], along_z(k))

    @pl.when(core == 1)
    def _():
        tell(pair_sem, at_ctx(partner))

    def factors_of(tops):
        top = functools.reduce(jnp.maximum, tops)
        return top, [jnp.exp(m - top) for m in tops]

    def z_copy(i, k, target):
        src, dst = (szs, rzs) if i == PIECES else (sz.at[i], rz.at[i])
        return pltpu.make_async_remote_copy(
            src_ref=src, dst_ref=dst.at[k], send_sem=sz_sem.at[i // PIECES], recv_sem=rz_sem.at[i],
            device_id=at_ctx(target), device_id_type=MESH,
        )

    arrived(rxs.at[six], rx_sem.at[PIECES])
    top, factors = factors_of([sxs[0, 0:1, :]] + [rxs[k, 0:1, :] for k in senders])
    total = factors[0] * sxs[0, 1:2, :]
    for n, k in enumerate(senders):
        total = total + factors[n + 1] * rxs[k, 1:2, :]

    @pl.when(core == 0)
    def _():
        pl.semaphore_wait(pair_sem, 1)

    @pl.when(~owns_odd)
    def _():
        szs[0:1, :] = top
        szs[1:2, :] = total
        z_copy(PIECES, z, owner).start()

    @pl.when(owns_odd)
    def _():
        rzs[OWNER_Z + 1, 0:1, :] = top
        rzs[OWNER_Z + 1, 1:2, :] = total

    for i in range(PIECES):
        arrived(rx.at[i, six], rx_sem.at[i])
        mix = factors[0] * sx[i, 0].astype(F32)
        for n, k in enumerate(senders):
            mix = mix + factors[n + 1] * rx[i, k].astype(F32)

        @pl.when(~owns_odd)
        def _():
            sz[i] = mix.astype(BF16)
            z_copy(i, z, owner).start()

        @pl.when(owns_odd)
        def _():
            rz[i, OWNER_Z + 1] = mix.astype(BF16)

    at_foot = (z == 0) & (core == 0)

    def anchor_up():
        @pl.when(x > 0)
        def _():
            anchor_copy(x, 0, c).wait_recv()

        for k in (7, 6, 5, 4, 3, 2, 1):
            anchor_copy(x, 1, k * 8 + g).start()

    pl.semaphore_wait(near_sem.at[2], 2)
    for k in (1, 15):
        tell(near_sem.at[3], along_z(k))

    @pl.when(at_foot)
    def _():
        anchor_up()

    def gz_copy(i, target):
        return pltpu.make_async_remote_copy(
            src_ref=owned.at[i], dst_ref=att.at[i, owned_head], send_sem=gzs_sem, recv_sem=gzr_sem.at[i],
            device_id=at_ctx(target), device_id_type=MESH,
        )

    def gx_copy(i, target):
        return pltpu.make_async_remote_copy(
            src_ref=att.at[i, g], dst_ref=att.at[i, g], send_sem=gxs_sem, recv_sem=gxr_sem.at[i],
            device_id=at_ctx(target), device_id_type=MESH,
        )

    def gx_send(i):
        for slot in (4, 5, 2, 3, 6, 7, 1):
            gx_copy(i, x_peer(slot // 2, slot % 2)).start()

    def column_arrived(ref, sem):
        @pl.when(owns_even)
        def _():
            arrived(ref, sem)

        @pl.when(owns_odd)
        def _():
            arrived(ref.at[others], sem)

    @pl.when(owns_even | owns_odd)
    def _():
        self_top, self_total, self_mix = self_part
        column_arrived(rzs, rz_sem.at[PIECES])
        _, parts = factors_of([self_top] + [rzs[k, 0:1, :] for k in range(NZ)])
        whole = parts[0] * self_total
        for k in range(NZ):
            whole = whole + parts[k + 1] * rzs[k, 1:2, :]
        for i in range(PIECES):
            column_arrived(rz.at[i], rz_sem.at[i])
            summed = parts[0] * self_mix[piece(i)]
            for k in range(NZ):
                summed = summed + parts[k + 1] * rz[i, k].astype(F32)
            owned[i] = (summed / whole).astype(BF16)

            @pl.when(owns_odd)
            def _():
                att[i, g] = owned[i]

            for k in (0, 1, 2, 7, 3, 6, 5):
                gz_copy(i, k * 8 + owned_head).start()

            @pl.when(owns_even)
            def _():
                gz_copy(i, 4 * 8 + owned_head).start()

    @pl.when(owns_odd)
    def _():
        for i in range(PIECES):
            gx_send(i)

    @pl.when(~owns_odd)
    def _():
        for i in range(PIECES):
            arrived(att.at[i, 0], gzr_sem.at[i])
            gx_send(i)

    pl.semaphore_wait(near_sem.at[3], 2)
    arrived(cq_v, in_sem.at[5])

    projected = None
    for i in range(PIECES):
        arrived(att.at[i, others], gxr_sem.at[i])
        share = nn(wt[i], att[i].reshape(GROUPS * PIECE, ROWS))
        projected = share if projected is None else projected + share
    hs[...] = projected.T.astype(BF16).reshape(8, 16, HEAD)

    def h_copy(slot, source, target):
        return pltpu.make_async_remote_copy(
            src_ref=hs.at[source], dst_ref=hr.at[slot], send_sem=hs_sem, recv_sem=hr_sem,
            device_id={"ctx": c, "head": target}, device_id_type=MESH,
        )

    for slot in (6, 5, 7, 4, 2, 1, 3):
        peer = head_peer(slot // 4, slot % 4)
        h_copy(slot, peer, peer).start()

    @pl.when(core == 0)
    def _():
        @pl.when(z > 0)
        def _():
            anchor_copy(x, 0, c).wait_recv()

        for k in (2, 1, 3):

            @pl.when((z > 0) | ((x + k) % 4 > 0))
            def _():
                anchor_copy(x, 2, z * 8 + ((x + k) % 4) * 2).start()

        anchor_copy(x, 3, c + 1).start()

    @pl.when((core == 0) & (c > 0))
    def _():
        for k in (1, 3, 2):
            q = (x + k) % 4
            anchor_copy(q, 0, c).wait_recv()
            anchor_copy(q, 3, c + 1).start()

    @pl.when(c == 0)
    def _():
        for q in range(1, 4):
            anchor_copy(q, 3, 1).start()

    @pl.when(core == 1)
    def _():
        for q in range(4):
            anchor_copy(q, 0, c).wait_recv()

    off = jnp.where(c > 0, 0.0, FAR).astype(F32)
    k_all = kv[0]
    v_all = jnp.concatenate([kv[1], jnp.ones((2 * BLOCK, HEAD), BF16)], axis=1)
    tri = lax.broadcasted_iota(jnp.int32, (ROWS, ROWS), 0) >= lax.broadcasted_iota(jnp.int32, (ROWS, ROWS), 1)
    for j in range(GROUPS):
        for half in range(2):
            r0 = half * ROWS
            seen = BLOCK + r0 + ROWS
            q = cq_v[r0 : r0 + ROWS, j * HEAD : (j + 1) * HEAD]
            s = nt(q, k_all[:seen]) * SCALE
            pieces = [s[:, :BLOCK] + off]
            if half:
                pieces.append(s[:, BLOCK : BLOCK + ROWS])
            pieces.append(jnp.where(tri, s[:, seen - ROWS :], FAR))
            s = jnp.concatenate(pieces, axis=1)
            m = jnp.max(s, axis=1, keepdims=True)
            p = jnp.exp(s - m).astype(BF16)
            r = nn(p, v_all[:seen])
            co_v[r0 : r0 + ROWS, j * HEAD : (j + 1) * HEAD] = (r[:, :HEAD] / r[:, HEAD:]).astype(BF16)
        if j % 2:
            cols = slice((j - 1) * HEAD, (j + 1) * HEAD)
            pltpu.make_async_copy(co_v.at[:, cols], ctx_out.at[:, cols], out_sem).start()

    arrived(co_v, out_sem)
    arrived(sxs.at[six], sx_sem.at[1])
    arrived(pxs, sp_sem.at[1])
    arrived(hs.at[others], hs_sem)
    arrived(sx.at[:, six], sx_sem.at[0])
    arrived(px, sp_sem.at[0])
    arrived(att.at[:, others], gxs_sem)

    @pl.when(~owns_odd)
    def _():
        arrived(szs, sz_sem.at[1])
        arrived(sz, sz_sem.at[0])

    @pl.when(owns_even)
    def _():
        arrived(att, gzs_sem)

    @pl.when(owns_odd)
    def _():
        arrived(att.at[:, others], gzs_sem)

    @pl.when(c == 0)
    def _():
        anchor_sent(0, 3)

    @pl.when(at_foot)
    def _():
        anchor_sent(1, 7)

    @pl.when(core == 0)
    def _():
        @pl.when((z == 0) & (x > 0))
        def _():
            anchor_sent(2, 2)

        @pl.when((z > 0) | (x == 0))
        def _():
            anchor_sent(2, 3)

        anchor_sent(3, 4)

    arrived(hr.at[others], hr_sem)
    result = hs[h].astype(F32)
    for slot in range(1, 8):
        result = result + hr[slot].astype(F32)
    opt_out[...] = result.astype(BF16)


def put_out(co, oo, ctx_out, opt_out, sem):
    copies = [pltpu.make_async_copy(oo, opt_out, sem.at[0]), pltpu.make_async_copy(co, ctx_out, sem.at[1])]
    for copy in copies:
        copy.start()
    for copy in copies:
        copy.wait()


def layer(cq, ck, cv, oq, ok, ov, seg, w):
    vmem, dma = pltpu.VMEM, pltpu.SemaphoreType.DMA
    anywhere = pl.BlockSpec(memory_space=pl.ANY)
    parts = pl.pallas_call(
        kernel,
        name="star_attention",
        out_shape=(vmem((BLOCK, GROUPS * HEAD), BF16), vmem((ROWS // 8, HEAD), BF16)),
        in_specs=[anywhere] * 8,
        out_specs=(anywhere, pl.BlockSpec(memory_space=vmem)),
        scratch_shapes=[
            vmem((BLOCK, GROUPS * HEAD), BF16),
            vmem((2, 2 * BLOCK, HEAD), BF16),
            vmem((BLOCK, GROUPS * HEAD), BF16),
            vmem((ROWS, GROUPS * HEAD), BF16),
            vmem((ROWS, HEAD), BF16),
            vmem((ROWS, HEAD), BF16),
            vmem((1, ROWS), jnp.int32),
            vmem((GROUPS * HEAD, HEAD), BF16),
            vmem((PIECES, HEAD, GROUPS * PIECE), BF16),
            vmem((PIECES, 8, PIECE, ROWS), BF16),
            vmem((8, 2, ROWS), F32),
            vmem((PIECES, PIECE, ROWS), BF16),
            vmem((2, ROWS), F32),
            vmem((PIECES, 8, PIECE, ROWS), BF16),
            vmem((8, 2, ROWS), F32),
            vmem((PIECES, PIECE, ROWS), BF16),
            vmem((2, ROWS), F32),
            vmem((PIECES, 8, PIECE, ROWS), BF16),
            vmem((8, 2, ROWS), F32),
            vmem((PIECES, PIECE, ROWS), BF16),
            vmem((PIECES, 8, PIECE, ROWS), BF16),
            vmem((8, 16, HEAD), BF16),
            vmem((8, 16, HEAD), BF16),
            dma((7,)),
            dma(()),
            dma((2,)),
            dma((2,)),
            dma((2,)),
            dma((PIECES + 1,)),
            dma((2,)),
            dma((PIECES + 1,)),
            dma(()),
            dma((PIECES,)),
            dma(()),
            dma((PIECES,)),
            dma(()),
            dma(()),
            dma((4,)),
            dma((4,)),
            pltpu.SemaphoreType.REGULAR((4,)),
            pltpu.SemaphoreType.REGULAR,
        ],
        compiler_params=pltpu.CompilerParams(collective_id=0, has_side_effects=True),
    )(cq, ck, cv, oq, ok, ov, seg.reshape(1, ROWS), w)
    return pl.pallas_call(
        put_out,
        name="put_out",
        out_shape=(
            jax.ShapeDtypeStruct((BLOCK, GROUPS * HEAD), BF16),
            jax.ShapeDtypeStruct((ROWS // 8, HEAD), BF16),
        ),
        in_specs=[pl.BlockSpec(memory_space=vmem)] * 2,
        out_specs=(anywhere, anywhere),
        scratch_shapes=[dma((2,))],
    )(*[pltpu.with_memory_space_constraint(part, vmem) for part in parts])


def solution(mesh):
    placed = (
        P("ctx", "head"),
        P("ctx", "head"),
        P("ctx", "head"),
        P(None, "head"),
        P(None, "head"),
        P(None, "head"),
        P(),
        P("head", "ctx"),
    )
    return jax.shard_map(
        layer,
        mesh=mesh,
        in_specs=placed,
        out_specs=(P("ctx", "head"), P("head", "ctx")),
        check_vma=False,
    )
```

```python
import functools

import jax
import jax.numpy as jnp
from jax import lax
from jax.experimental import pallas as pl
from jax.experimental.pallas import tpu as pltpu
from jax.sharding import PartitionSpec as P

MESH = pl.DeviceIdType.MESH
HEAD = 128
ROWS = 128
BLOCK = 256
GROUPS = 8
NZ = 8
OWNER_Z = 3
PIECES = 4
PIECE = HEAD // PIECES
QUARTER = BLOCK // 4
SCALE = HEAD ** (-0.5)
FAR = -1e30
F32 = jnp.float32
BF16 = jnp.bfloat16


def nt(a, b):
    return lax.dot_general(a, b, (((1,), (1,)), ((), ())), preferred_element_type=F32)


def nn(a, b):
    return lax.dot_general(a, b, (((1,), (0,)), ((), ())), preferred_element_type=F32)


def kernel(
    cq, ck, cv, oq, ok, ov, seg, w,
    ctx_out, opt_out,
    cq_v, kv, co_v, oq_v, ok_v, ov_v, seg_v, w_v, wt,
    sx, sxs, px, pxs, rx, rxs, sz, szs, rz, rzs, owned, att, hs, hr,
    in_sem, out_sem, sp_sem, rp_sem, sx_sem, rx_sem, sz_sem, rz_sem,
    gzs_sem, gzr_sem, gxs_sem, gxr_sem, hs_sem, hr_sem, as_sem, ar_sem, near_sem, pair_sem,
):
    c = lax.axis_index("ctx")
    h = lax.axis_index("head")
    z, g = c // 8, c % 8
    x, core = g // 2, g % 2
    zh, y = h // 4, h % 4
    zo = OWNER_Z + core
    owner = zo * 8 + x * 2 + 1
    partner = z * 8 + x * 2 + (core + 1) % 2
    owns_even = (core == 1) & (z == OWNER_Z)
    owns_odd = (core == 1) & (z == OWNER_Z + 1)
    owned_head = x * 2 + (z + OWNER_Z) % 2

    def at_ctx(cc):
        return {"ctx": cc, "head": h}

    def x_peer(dx, dc):
        return z * 8 + ((x + dx) % 4) * 2 + (core + dc) % 2

    def head_peer(kz, ky):
        return ((zh + kz) % 2) * 4 + (y + ky) % 4

    def along_z(k):
        zz = (zh * NZ + z + k) % (2 * NZ)
        return {"ctx": (zz % NZ) * 8 + g, "head": (zz // NZ) * 4 + y}

    def tell(sem, target):
        pl.semaphore_signal(sem, inc=1, device_id=target, device_id_type=MESH)

    own = pl.ds(BLOCK, BLOCK)
    anchor = pl.ds(0, BLOCK)
    def arrived(ref, sem):
        pltpu.make_async_copy(ref, ref, sem).wait()

    def query_load(dx):
        cols = pl.ds(pl.multiple_of(((x + dx) % 4) * 2 * HEAD, 2 * HEAD), 2 * HEAD)
        return pltpu.make_async_copy(oq.at[:, cols], oq_v.at[:, cols], in_sem.at[0 if dx == 2 else 1])

    pltpu.make_async_copy(ck, kv.at[0, own], in_sem.at[0]).start()
    query_load(2).start()
    pltpu.make_async_copy(cv, kv.at[1, own], in_sem.at[0]).start()
    barrier = pltpu.get_barrier_semaphore()
    for slot in range(1, 8):
        tell(barrier, at_ctx(x_peer(slot // 2, slot % 2)))
    for k in (1, 15):
        tell(barrier, along_z(k))
    for k in range(1, 4):
        tell(barrier, {"ctx": c, "head": head_peer(0, k)})
    for dx in (1, 3, 0):
        query_load(dx).start()
    pltpu.make_async_copy(ok, ok_v, in_sem.at[2]).start()
    pltpu.make_async_copy(ov, ov_v, in_sem.at[2]).start()
    pltpu.make_async_copy(seg, seg_v, in_sem.at[3]).start()
    pltpu.make_async_copy(w, w_v, in_sem.at[4]).start()
    pltpu.make_async_copy(cq, cq_v, in_sem.at[5]).start()

    @pl.when(c == 0)
    def _():
        pltpu.make_async_copy(ck, kv.at[0, anchor], in_sem.at[6]).start()
        pltpu.make_async_copy(cv, kv.at[1, anchor], in_sem.at[6]).start()

    def anchor_copy(q, n, target):
        ref = kv.at[:, pl.ds(pl.multiple_of(q * QUARTER, QUARTER), QUARTER)]
        return pltpu.make_async_remote_copy(
            src_ref=ref, dst_ref=ref, send_sem=as_sem.at[n], recv_sem=ar_sem.at[q],
            device_id=at_ctx(target), device_id_type=MESH,
        )

    def anchor_sent(n, quarters):
        arrived(kv.at[:, 0 : quarters * QUARTER], as_sem.at[n])

    arrived(oq_v.at[:, 0 : 6 * HEAD], in_sem.at[0])
    k_own = kv[0, own, :]
    vt_own = kv[1, own, :].astype(F32).T.astype(BF16)

    def partial(q, keys, vt, mask=None):
        s = nt(keys, q) * SCALE
        if mask is not None:
            s = jnp.where(mask, s, FAR)
        m = jnp.max(s, axis=0, keepdims=True)
        p = jnp.exp(s - m)
        if mask is not None:
            p = jnp.where(mask, p, 0.0)
        return m, jnp.sum(p, axis=0, keepdims=True), nn(vt, p.astype(BF16))

    def x_copy(i, slot, target):
        src, dst = (sxs, rxs) if i == PIECES else (sx.at[i], rx.at[i])
        return pltpu.make_async_remote_copy(
            src_ref=src.at[slot], dst_ref=dst.at[slot],
            send_sem=sx_sem.at[i // PIECES], recv_sem=rx_sem.at[i],
            device_id=at_ctx(target), device_id_type=MESH,
        )

    others = pl.ds(1, 7)
    six = pl.ds(1, 6)
    senders = (1, 2, 3, 4, 6, 7)

    def piece(i):
        return slice(i * PIECE, (i + 1) * PIECE)

    def option_heads(slots):
        qs = []
        for slot in slots:
            gd = ((x + slot // 2) % 4) * 2 + (core + slot % 2) % 2
            qs.append(oq_v[:, pl.ds(pl.multiple_of(gd * HEAD, HEAD), HEAD)])
        m, l, mix = partial(jnp.concatenate(qs, axis=0), k_own, vt_own)
        for n, slot in enumerate(slots):
            lanes = slice(n * ROWS, (n + 1) * ROWS)
            for i in range(PIECES):
                sx[i, slot] = mix[piece(i), lanes].astype(BF16)
            sxs[slot, 0:1, :] = m[:, lanes]
            sxs[slot, 1:2, :] = l[:, lanes]

    def send_heads(i, slots):
        for slot in slots:
            x_copy(i, slot, x_peer(slot // 2, slot % 2)).start()

    def pair_copy(i):
        src, dst = (sxs, pxs) if i == PIECES else (sx.at[i], px.at[i])
        return pltpu.make_async_remote_copy(
            src_ref=src.at[5], dst_ref=dst, send_sem=sp_sem.at[i // PIECES], recv_sem=rp_sem.at[i // PIECES],
            device_id=at_ctx(partner), device_id_type=MESH,
        )

    option_heads((5, 4))
    pl.semaphore_wait(barrier, 12)
    for i in (PIECES, *range(PIECES)):
        pair_copy(i).start()
    for k in (1, 15):
        tell(near_sem.at[0], along_z(k))

    arrived(oq_v.at[:, 0 : 6 * HEAD], in_sem.at[1])
    option_heads((2, 3, 6, 7))
    send_heads(PIECES, (2, 3, 6, 7))
    send_heads(0, (2, 3, 6, 7))

    option_heads((1, 0))
    send_heads(PIECES, (1,))
    send_heads(0, (1,))

    arrived(pxs, rp_sem.at[1])
    m_here, m_there = sxs[4, 0:1, :], pxs[0:1, :]
    m_pair = jnp.maximum(m_here, m_there)
    f_here, f_there = jnp.exp(m_here - m_pair), jnp.exp(m_there - m_pair)
    l_pair = f_here * sxs[4, 1:2, :] + f_there * pxs[1:2, :]
    sxs[4, 0:1, :] = m_pair
    sxs[4, 1:2, :] = l_pair
    arrived(px, rp_sem.at[0])
    for i in range(PIECES):
        sx[i, 4] = (f_here * sx[i, 4].astype(F32) + f_there * px[i].astype(F32)).astype(BF16)
    send_heads(PIECES, (4,))
    send_heads(0, (4,))
    for i in range(1, PIECES):
        send_heads(i, (4, 2, 3, 6, 7, 1))

    @pl.when(c == 0)
    def _():
        arrived(kv.at[:, anchor], in_sem.at[6])
        for q in (2, 1, 3):
            anchor_copy(q, 0, q * 2).start()

    pl.semaphore_wait(near_sem.at[0], 2)
    for k in (2, 14):
        tell(near_sem.at[1], along_z(k))

    arrived(kv.at[0, own], in_sem.at[2])
    arrived(seg_v, in_sem.at[3])
    seg_row = jnp.broadcast_to(seg_v[...].astype(F32), (ROWS, ROWS))
    seg_col = seg_row.T
    key_at = lax.broadcasted_iota(jnp.int32, (ROWS, ROWS), 0)
    row_at = lax.broadcasted_iota(jnp.int32, (ROWS, ROWS), 1)
    visible = (seg_row == seg_col) & (row_at >= key_at)
    q_own = oq_v[:, pl.ds(pl.multiple_of(owned_head * HEAD, HEAD), HEAD)]
    vt_self = ov_v[...].astype(F32).T.astype(BF16)
    self_part = partial(q_own, ok_v[...], vt_self, visible)

    arrived(w_v, in_sem.at[4])
    for i in range(PIECES):
        rows = [w_v[j * HEAD + i * PIECE : j * HEAD + (i + 1) * PIECE, :] for j in range(GROUPS)]
        wt[i] = jnp.concatenate(rows, axis=0).astype(F32).T.astype(BF16)

    pl.semaphore_wait(near_sem.at[1], 2)
    for k in (4, 12):
        tell(near_sem.at[2], along_z(k))

    @pl.when(core == 1)
    def _():
        tell(pair_sem, at_ctx(partner))

    def factors_of(tops):
        top = functools.reduce(jnp.maximum, tops)
        return top, [jnp.exp(m - top) for m in tops]

    def z_copy(i, k, target):
        src, dst = (szs, rzs) if i == PIECES else (sz.at[i], rz.at[i])
        return pltpu.make_async_remote_copy(
            src_ref=src, dst_ref=dst.at[k], send_sem=sz_sem.at[i // PIECES], recv_sem=rz_sem.at[i],
            device_id=at_ctx(target), device_id_type=MESH,
        )

    arrived(rxs.at[six], rx_sem.at[PIECES])
    top, factors = factors_of([sxs[0, 0:1, :]] + [rxs[k, 0:1, :] for k in senders])
    total = factors[0] * sxs[0, 1:2, :]
    for n, k in enumerate(senders):
        total = total + factors[n + 1] * rxs[k, 1:2, :]

    @pl.when(core == 0)
    def _():
        pl.semaphore_wait(pair_sem, 1)

    @pl.when(~owns_odd)
    def _():
        szs[0:1, :] = top
        szs[1:2, :] = total
        z_copy(PIECES, z, owner).start()

    @pl.when(owns_odd)
    def _():
        rzs[OWNER_Z + 1, 0:1, :] = top
        rzs[OWNER_Z + 1, 1:2, :] = total

    for i in range(PIECES):
        arrived(rx.at[i, six], rx_sem.at[i])
        mix = factors[0] * sx[i, 0].astype(F32)
        for n, k in enumerate(senders):
            mix = mix + factors[n + 1] * rx[i, k].astype(F32)

        @pl.when(~owns_odd)
        def _():
            sz[i] = mix.astype(BF16)
            z_copy(i, z, owner).start()

        @pl.when(owns_odd)
        def _():
            rz[i, OWNER_Z + 1] = mix.astype(BF16)

    at_foot = (z == 0) & (core == 0)

    def anchor_up():
        @pl.when(x > 0)
        def _():
            anchor_copy(x, 0, c).wait_recv()

        for k in (7, 6, 5, 4, 3, 2, 1):
            anchor_copy(x, 1, k * 8 + g).start()

    pl.semaphore_wait(near_sem.at[2], 2)
    for k in (1, 15):
        tell(near_sem.at[3], along_z(k))

    @pl.when(at_foot)
    def _():
        anchor_up()

    def gz_copy(i, target):
        return pltpu.make_async_remote_copy(
            src_ref=owned.at[i], dst_ref=att.at[i, owned_head], send_sem=gzs_sem, recv_sem=gzr_sem.at[i],
            device_id=at_ctx(target), device_id_type=MESH,
        )

    def gx_copy(i, target):
        return pltpu.make_async_remote_copy(
            src_ref=att.at[i, g], dst_ref=att.at[i, g], send_sem=gxs_sem, recv_sem=gxr_sem.at[i],
            device_id=at_ctx(target), device_id_type=MESH,
        )

    def gx_send(i):
        for slot in (4, 5, 2, 3, 6, 7, 1):
            gx_copy(i, x_peer(slot // 2, slot % 2)).start()

    def column_arrived(ref, sem):
        @pl.when(owns_even)
        def _():
            arrived(ref, sem)

        @pl.when(owns_odd)
        def _():
            arrived(ref.at[others], sem)

    @pl.when(owns_even | owns_odd)
    def _():
        self_top, self_total, self_mix = self_part
        column_arrived(rzs, rz_sem.at[PIECES])
        _, parts = factors_of([self_top] + [rzs[k, 0:1, :] for k in range(NZ)])
        whole = parts[0] * self_total
        for k in range(NZ):
            whole = whole + parts[k + 1] * rzs[k, 1:2, :]
        for i in range(PIECES):
            column_arrived(rz.at[i], rz_sem.at[i])
            summed = parts[0] * self_mix[piece(i)]
            for k in range(NZ):
                summed = summed + parts[k + 1] * rz[i, k].astype(F32)
            owned[i] = (summed / whole).astype(BF16)

            @pl.when(owns_odd)
            def _():
                att[i, g] = owned[i]

            for k in (0, 1, 2, 7, 3, 6, 5):
                gz_copy(i, k * 8 + owned_head).start()

            @pl.when(owns_even)
            def _():
                gz_copy(i, 4 * 8 + owned_head).start()

    @pl.when(owns_odd)
    def _():
        for i in range(PIECES):
            gx_send(i)

    @pl.when(~owns_odd)
    def _():
        for i in range(PIECES):
            arrived(att.at[i, 0], gzr_sem.at[i])
            gx_send(i)

    pl.semaphore_wait(near_sem.at[3], 2)
    arrived(cq_v, in_sem.at[5])

    projected = None
    for i in range(PIECES):
        arrived(att.at[i, others], gxr_sem.at[i])
        share = nn(wt[i], att[i].reshape(GROUPS * PIECE, ROWS))
        projected = share if projected is None else projected + share
    hs[...] = projected.T.astype(BF16).reshape(8, 16, HEAD)

    def h_copy(slot, source, target):
        return pltpu.make_async_remote_copy(
            src_ref=hs.at[source], dst_ref=hr.at[slot], send_sem=hs_sem, recv_sem=hr_sem,
            device_id={"ctx": c, "head": target}, device_id_type=MESH,
        )

    for slot in (6, 5, 7, 4, 2, 1, 3):
        peer = head_peer(slot // 4, slot % 4)
        h_copy(slot, peer, peer).start()

    @pl.when(core == 0)
    def _():
        @pl.when(z > 0)
        def _():
            anchor_copy(x, 0, c).wait_recv()

        for k in (2, 1, 3):

            @pl.when((z > 0) | ((x + k) % 4 > 0))
            def _():
                anchor_copy(x, 2, z * 8 + ((x + k) % 4) * 2).start()

        anchor_copy(x, 3, c + 1).start()

    @pl.when((core == 0) & (c > 0))
    def _():
        for k in (1, 3, 2):
            q = (x + k) % 4
            anchor_copy(q, 0, c).wait_recv()
            anchor_copy(q, 3, c + 1).start()

    @pl.when(c == 0)
    def _():
        for q in range(1, 4):
            anchor_copy(q, 3, 1).start()

    @pl.when(core == 1)
    def _():
        for q in range(4):
            anchor_copy(q, 0, c).wait_recv()

    off = jnp.where(c > 0, 0.0, FAR).astype(F32)
    k_all = kv[0]
    v_all = jnp.concatenate([kv[1], jnp.ones((2 * BLOCK, HEAD), BF16)], axis=1)
    tri = lax.broadcasted_iota(jnp.int32, (ROWS, ROWS), 0) >= lax.broadcasted_iota(jnp.int32, (ROWS, ROWS), 1)
    for j in range(GROUPS):
        for half in range(2):
            r0 = half * ROWS
            seen = BLOCK + r0 + ROWS
            q = cq_v[r0 : r0 + ROWS, j * HEAD : (j + 1) * HEAD]
            s = nt(q, k_all[:seen]) * SCALE
            pieces = [s[:, :BLOCK] + off]
            if half:
                pieces.append(s[:, BLOCK : BLOCK + ROWS])
            pieces.append(jnp.where(tri, s[:, seen - ROWS :], FAR))
            s = jnp.concatenate(pieces, axis=1)
            m = jnp.max(s, axis=1, keepdims=True)
            p = jnp.exp(s - m).astype(BF16)
            r = nn(p, v_all[:seen])
            co_v[r0 : r0 + ROWS, j * HEAD : (j + 1) * HEAD] = (r[:, :HEAD] / r[:, HEAD:]).astype(BF16)
        if j % 2:
            cols = slice((j - 1) * HEAD, (j + 1) * HEAD)
            pltpu.make_async_copy(co_v.at[:, cols], ctx_out.at[:, cols], out_sem).start()

    arrived(co_v, out_sem)
    arrived(sxs.at[six], sx_sem.at[1])
    arrived(pxs, sp_sem.at[1])
    arrived(hs.at[others], hs_sem)
    arrived(sx.at[:, six], sx_sem.at[0])
    arrived(px, sp_sem.at[0])
    arrived(att.at[:, others], gxs_sem)

    @pl.when(~owns_odd)
    def _():
        arrived(szs, sz_sem.at[1])
        arrived(sz, sz_sem.at[0])

    @pl.when(owns_even)
    def _():
        arrived(att, gzs_sem)

    @pl.when(owns_odd)
    def _():
        arrived(att.at[:, others], gzs_sem)

    @pl.when(c == 0)
    def _():
        anchor_sent(0, 3)

    @pl.when(at_foot)
    def _():
        anchor_sent(1, 7)

    @pl.when(core == 0)
    def _():
        @pl.when((z == 0) & (x > 0))
        def _():
            anchor_sent(2, 2)

        @pl.when((z > 0) | (x == 0))
        def _():
            anchor_sent(2, 3)

        anchor_sent(3, 4)

    arrived(hr.at[others], hr_sem)
    result = hs[h].astype(F32)
    for slot in range(1, 8):
        result = result + hr[slot].astype(F32)
    opt_out[...] = result.astype(BF16)


def put_out(co, oo, ctx_out, opt_out, sem):
    copies = [pltpu.make_async_copy(oo, opt_out, sem.at[0]), pltpu.make_async_copy(co, ctx_out, sem.at[1])]
    for copy in copies:
        copy.start()
    for copy in copies:
        copy.wait()


def layer(cq, ck, cv, oq, ok, ov, seg, w):
    vmem, dma = pltpu.VMEM, pltpu.SemaphoreType.DMA
    anywhere = pl.BlockSpec(memory_space=pl.ANY)
    parts = pl.pallas_call(
        kernel,
        name="star_attention",
        out_shape=(vmem((BLOCK, GROUPS * HEAD), BF16), vmem((ROWS // 8, HEAD), BF16)),
        in_specs=[anywhere] * 8,
        out_specs=(anywhere, pl.BlockSpec(memory_space=vmem)),
        scratch_shapes=[
            vmem((BLOCK, GROUPS * HEAD), BF16),
            vmem((2, 2 * BLOCK, HEAD), BF16),
            vmem((BLOCK, GROUPS * HEAD), BF16),
            vmem((ROWS, GROUPS * HEAD), BF16),
            vmem((ROWS, HEAD), BF16),
            vmem((ROWS, HEAD), BF16),
            vmem((1, ROWS), jnp.int32),
            vmem((GROUPS * HEAD, HEAD), BF16),
            vmem((PIECES, HEAD, GROUPS * PIECE), BF16),
            vmem((PIECES, 8, PIECE, ROWS), BF16),
            vmem((8, 2, ROWS), F32),
            vmem((PIECES, PIECE, ROWS), BF16),
            vmem((2, ROWS), F32),
            vmem((PIECES, 8, PIECE, ROWS), BF16),
            vmem((8, 2, ROWS), F32),
            vmem((PIECES, PIECE, ROWS), BF16),
            vmem((2, ROWS), F32),
            vmem((PIECES, 8, PIECE, ROWS), BF16),
            vmem((8, 2, ROWS), F32),
            vmem((PIECES, PIECE, ROWS), BF16),
            vmem((PIECES, 8, PIECE, ROWS), BF16),
            vmem((8, 16, HEAD), BF16),
            vmem((8, 16, HEAD), BF16),
            dma((7,)),
            dma(()),
            dma((2,)),
            dma((2,)),
            dma((2,)),
            dma((PIECES + 1,)),
            dma((2,)),
            dma((PIECES + 1,)),
            dma(()),
            dma((PIECES,)),
            dma(()),
            dma((PIECES,)),
            dma(()),
            dma(()),
            dma((4,)),
            dma((4,)),
            pltpu.SemaphoreType.REGULAR((4,)),
            pltpu.SemaphoreType.REGULAR,
        ],
        compiler_params=pltpu.CompilerParams(collective_id=0, has_side_effects=True),
    )(cq, ck, cv, oq, ok, ov, seg.reshape(1, ROWS), w)
    return pl.pallas_call(
        put_out,
        name="put_out",
        out_shape=(
            jax.ShapeDtypeStruct((BLOCK, GROUPS * HEAD), BF16),
            jax.ShapeDtypeStruct((ROWS // 8, HEAD), BF16),
        ),
        in_specs=[pl.BlockSpec(memory_space=vmem)] * 2,
        out_specs=(anywhere, anywhere),
        scratch_shapes=[dma((2,))],
    )(*[pltpu.with_memory_space_constraint(part, vmem) for part in parts])


def solution(mesh):
    placed = (
        P("ctx", "head"),
        P("ctx", "head"),
        P("ctx", "head"),
        P(None, "head"),
        P(None, "head"),
        P(None, "head"),
        P(),
        P("head", "ctx"),
    )
    return jax.shard_map(
        layer,
        mesh=mesh,
        in_specs=placed,
        out_specs=(P("ctx", "head"), P("head", "ctx")),
        check_vma=False,
    )
```
